32 devices in a mesh: var: 8 (over y, x, core), tp: 4 (over z).
Axes of the slice: x: 2, y: 2, z: 4, core: 2. Of those that a mesh axis runs over, the one named last changes fastest.
Arguments:
- tokens: bfloat16 [8192, 8192], P('var', 'tp'), may hold values from -6 to 6
- kv_weight: bfloat16 [8192, 2048], P('tp'), may hold values from -0.0625 to 0.0625
- factor_a: bfloat16 [16, 8192, 128], P('var', 'tp'), may hold values from -0.0625 to 0.0625
- factor_scale: bfloat16 [16, 128], P('var'), may hold values from 0.29882812 to 3
- factor_b: bfloat16 [16, 128, 2048], P('var', None, 'tp'), may hold values from -0.5 to 0.5
- counts: int32 [8, 16], replicated, may hold values from 0 to 256, as said below
Outputs:
- kv_out: bfloat16 [8192, 2048], P('var', 'tp')
The draws below stay inside these ranges and needn't reach their ends.
Inputs may be any that keep to these rules, and one draw needn't show every extreme that they name: `counts`: each row sums to 1024. Owner o holds variants 2 * o to 2 * o + 1; in every row those variants together have at most 256 tokens, and in every draw one owner has exactly 256 tokens in every row.
All inputs are finite; a program needn't handle non-finite values.
Results may differ from the reference program's by a relative error of at most 0.011.
Values may be sent and summed in bfloat16 or wider, within the bound.
A program may use at most 128 MiB of HBM per device.

```python
import math
import jax
import jax.numpy as jnp
from jax import lax

D = 8192
R = 128
VAR_DEV = 2
TOK_GRP = 1024
KVW = 2048
GROUPS = 8
VARIANTS = 16
CAP = 256
TOKENS = 8192


def draw_counts(key, part):
    folded = jax.random.fold_in(key, 7)
    subkeys = jax.random.split(folded, 5)
    popular = jax.random.permutation(subkeys[0], GROUPS)
    orders = jax.vmap(lambda subkey: jax.random.permutation(subkey, GROUPS))(jax.random.split(subkeys[1], GROUPS))
    pair_count = GROUPS // 2
    first_owner = orders[:, 0::2]
    second_owner = orders[:, 1::2]
    pop_first = popular[first_owner]
    pop_second = popular[second_owner]
    draw_one = jax.random.randint(subkeys[2], (GROUPS, pair_count), 0, CAP + 1)
    draw_two = jax.random.randint(subkeys[3], (GROUPS, pair_count), 0, CAP + 1)
    strong = jnp.maximum(draw_one, draw_two)
    first_share = jnp.where(pop_first > pop_second, strong, CAP - strong)
    first_share = jnp.where(pop_first == GROUPS - 1, CAP, first_share)
    first_share = jnp.where(pop_second == GROUPS - 1, 0, first_share)
    row_ids = jnp.arange(GROUPS)[:, None]
    owner_loads = jnp.zeros((GROUPS, GROUPS), jnp.int32)
    owner_loads = owner_loads.at[row_ids, first_owner].set(first_share.astype(jnp.int32))
    owner_loads = owner_loads.at[row_ids, second_owner].set((CAP - first_share).astype(jnp.int32))
    first_part = jax.random.randint(subkeys[4], (GROUPS, GROUPS), 0, owner_loads + 1)
    forced = (row_ids == 0) & (popular[None, :] == GROUPS - 1)
    first_part = jnp.where(forced, owner_loads, first_part)
    split_counts = jnp.stack([first_part, owner_loads - first_part], axis=2)
    return split_counts.reshape(GROUPS, VARIANTS).astype(jnp.int32)


def block_levels(own_key, shape, cuts, smallest, top_value):
    loudness, own = 1.0, jax.random.fold_in(own_key, 6)
    for dim, shards_of in cuts:
        draws = jnp.exp(jax.random.uniform(jax.random.fold_in(own, dim), (shards_of,), jnp.float32, smallest / len(cuts), top_value / len(cuts)))
        loudness = loudness * jnp.repeat(draws, shape[dim] // shards_of).reshape([-1 if axis == dim else 1 for axis in range(len(shape))])
    return loudness


def noise(key, shape, spread, most, cuts=(), kind=jnp.bfloat16):
    array = spread * jax.random.normal(key, shape, jnp.float32)
    if cuts:
        array = array * block_levels(key, shape, cuts, -0.22, 0.18)
    return jnp.clip(array, -most, most).astype(kind)


def setup_inputs(seed: int = 0) -> dict:
    keys = jax.random.split(jax.random.key(seed), 7)
    tokens = noise(keys[0], (TOKENS, D), 1.0, 6.0, ((0, 8), (1, 4)))
    kv_weight = noise(keys[1], (D, KVW), D ** -0.5, 0.0625, ((0, 4),))
    factor_a = noise(keys[2], (VARIANTS, D, R), D ** -0.5, 0.0625, ((0, 8), (1, 4)))
    factor_scale = jnp.clip(jnp.exp(math.log(3.0) - 2.306499 * jax.random.uniform(keys[3], (VARIANTS, R), jnp.float32) ** block_levels(keys[3], (VARIANTS, R), ((0, 8),), -0.2, 0.2)), 0.29882812, 3.0).astype(jnp.bfloat16)
    factor_b = noise(keys[4], (VARIANTS, R, KVW), R ** -0.5, 0.5, ((0, 8), (2, 4)))
    counts = draw_counts(jax.random.fold_in(keys[6], 71), 0)
    return {"tokens": tokens, "kv_weight": kv_weight, "factor_a": factor_a, "factor_scale": factor_scale, "factor_b": factor_b, "counts": counts}


def owner_layout(group_counts):
    owner_counts = group_counts.reshape(GROUPS, VAR_DEV)
    starts = jnp.cumsum(group_counts) - group_counts
    first_rows = starts.reshape(GROUPS, VAR_DEV)[:, 0]
    slot_ids = jnp.arange(CAP, dtype=jnp.int32)
    filled = jnp.sum(owner_counts, axis=1)
    inside = slot_ids[None, :] < filled[:, None]
    bounds = jnp.cumsum(owner_counts, axis=1)
    local_pick = jnp.sum((slot_ids[None, :, None] >= bounds[:, None, :VAR_DEV - 1]).astype(jnp.int32), axis=2)
    picker = (local_pick[:, :, None] == jnp.arange(VAR_DEV, dtype=jnp.int32)[None, None, :]).astype(jnp.float32)
    return first_rows, inside, picker


def reference(tokens, kv_weight, factor_a, factor_scale, factor_b, counts):
    base_part = jnp.dot(tokens, kv_weight, preferred_element_type=jnp.float32)
    factor_in = factor_a.astype(jnp.float32).reshape(GROUPS, VAR_DEV, D, R)
    factor_out = factor_b.astype(jnp.float32).reshape(GROUPS, VAR_DEV, R, KVW)
    scale_table = factor_scale.astype(jnp.float32).reshape(GROUPS, VAR_DEV, R)[:, None]
    grouped = tokens.reshape(GROUPS, TOK_GRP, D)

    def one_group(inputs):
        group_tokens, group_counts = inputs
        first_rows, inside, picker = owner_layout(group_counts)
        slot_ids = jnp.arange(CAP, dtype=jnp.int32)
        row_index = jnp.clip(first_rows[:, None] + slot_ids[None, :], 0, TOK_GRP - 1).astype(jnp.int32)
        gathered = jnp.where(inside[:, :, None], group_tokens[row_index], jnp.zeros((), group_tokens.dtype))
        gathered = gathered.astype(jnp.float32)
        products = jnp.einsum("ocd,ovdr->ocvr", gathered, factor_in)
        rank_total = jnp.sum(products * picker[..., None], axis=2)
        scaled = rank_total * jnp.sum(picker[..., None] * scale_table, axis=2)
        scaled = lax.optimization_barrier(scaled.astype(jnp.bfloat16)).astype(jnp.float32)
        outputs = jnp.einsum("ocr,ovrk->ocvk", scaled, factor_out)
        delta_blocks = jnp.sum(outputs * picker[..., None], axis=2).astype(jnp.bfloat16)
        ends_at = jnp.cumsum(group_counts)
        position = jnp.arange(TOK_GRP, dtype=jnp.int32)
        variant = jnp.sum((ends_at[None, :] <= position[:, None]).astype(jnp.int32), axis=1)
        owner_of = variant // VAR_DEV
        owner_hot = owner_of[:, None] == jnp.arange(GROUPS, dtype=jnp.int32)[None, :]
        owner_first = jnp.sum(jnp.where(owner_hot, first_rows[None, :], 0), axis=1)
        flat_index = (owner_of * CAP + position - owner_first).astype(jnp.int32)
        return delta_blocks.reshape(GROUPS * CAP, KVW)[flat_index]

    delta_rows = lax.map(one_group, (grouped, counts)).reshape(TOKENS, KVW)
    return (base_part + delta_rows.astype(jnp.float32)).astype(jnp.bfloat16)
```

```python
import functools

import jax
import jax.numpy as jnp
from jax import lax
from jax.experimental import pallas as pl
from jax.experimental.pallas import tpu as pltpu
from jax.sharding import PartitionSpec as P

MESH = pl.DeviceIdType.MESH
PIECES = 4


def span(masks):
    found = [0]
    for mask in masks:
        found = found + [old ^ mask for old in found]
    return found


def kernel(
    V, K,
    tok_hbm, w_hbm, a_hbm, scale_ref, b_hbm, counts_ref,
    out_hbm,
    tok, w, a_all, b_raw, b_all, part, recv_up, recv_dn, rank, rank_up, rank_dn, rank_send_up,
    rank_send_dn, total, outv, ends,
    tok_sem, w_sem, own_sem, out_sem,
    a_send, a_recv, a_core_send, a_core_recv, b_send, b_recv, b_core_send, b_core_recv,
    up_send, up_recv, dn_send, dn_recv, rup_send, rup_recv, rdn_send, rdn_recv,
):
    v = lax.axis_index("var")
    p = lax.axis_index("tp")
    rows, feats = tok.shape
    cols = w.shape[2]
    var_dev = a_all.shape[1]
    R = a_all.shape[3]
    piece = rows // PIECES
    first, last = p == 0, p == K - 1
    low_half = p < K // 2

    def cut(i):
        return pl.ds(pl.multiple_of(i * piece, piece), piece)

    def chunk_at(k):
        c = k // 2
        c = jnp.where(k % 2 == 0, K - 1 - c, c)
        return jnp.where(low_half, c, K - 1 - c)

    def tok_copy(i):
        return pltpu.make_async_copy(tok_hbm.at[cut(i)], tok.at[cut(i)], tok_sem.at[i])

    def w_copy(k):
        c = chunk_at(k)
        return pltpu.make_async_copy(
            w_hbm.at[:, pl.ds(pl.multiple_of(c * cols, cols), cols)], w.at[c], w_sem.at[k]
        )

    tok_copy(0).start()
    w_copy(0).start()
    for i in range(1, PIECES):
        tok_copy(i).start()
    own_a = pltpu.make_async_copy(a_hbm, a_all.at[v], own_sem.at[0])
    own_b = pltpu.make_async_copy(b_hbm, b_raw, own_sem.at[1])
    own_a.start()
    own_b.start()
    for k in range(1, K):
        w_copy(k).start()

    masks = []
    m = 1
    while m < V:
        masks.append(m)
        m *= 2
    barrier = pltpu.get_barrier_semaphore()
    for m in masks:
        pl.semaphore_signal(barrier, inc=1, device_id=(lax.bitwise_xor(v, m), p), device_id_type=MESH)

    @pl.when(p > 0)
    def _():
        pl.semaphore_signal(barrier, inc=1, device_id=(v, p - 1), device_id_type=MESH)

    @pl.when(p < K - 1)
    def _():
        pl.semaphore_signal(barrier, inc=1, device_id=(v, p + 1), device_id_type=MESH)

    def base(c, i):
        part[c, cut(i)] = jnp.dot(
            tok[cut(i)], w[c], preferred_element_type=jnp.float32
        ).astype(jnp.bfloat16)

    w_copy(0).wait()
    tok_copy(0).wait()
    base(chunk_at(0), 0)

    pl.semaphore_wait(
        barrier, len(masks) + (p > 0).astype(jnp.int32) + (p < K - 1).astype(jnp.int32)
    )

    chips = masks[1:]
    orders = (chips, chips[::-1])

    def half(ref, h):
        size = ref.shape[1] // 2
        return ref.at[:, pl.ds(h * size, size)]

    pending = []

    class Gather:
        def __init__(self, own, everything, send, recv, core_send, core_recv):
            self.own, self.all = own, everything
            self.send, self.recv, self.core_send, self.core_recv = send, recv, core_send, core_recv
            self.used = 0

        def block(self, d, h):
            if d == 0 and self.own is not None:
                return half(self.own, h)
            return half(self.all.at[lax.bitwise_xor(v, d)], h)

        def to_chip(self, d, h, k):
            m = orders[h][k]
            copy = pltpu.make_async_remote_copy(
                src_ref=self.block(d, h),
                dst_ref=half(self.all.at[lax.bitwise_xor(v, d)], h),
                send_sem=self.send.at[self.used],
                recv_sem=self.recv.at[h, (d ^ m) // 2],
                device_id=(lax.bitwise_xor(v, m), p),
                device_id_type=MESH,
            )
            self.used += 1
            copy.start()
            pending.append(copy)

        def core_copy(self, d, h):
            return pltpu.make_async_remote_copy(
                src_ref=self.block(d, h),
                dst_ref=half(self.all.at[lax.bitwise_xor(v, d)], h),
                send_sem=self.core_send.at[h, d // 2],
                recv_sem=self.core_recv.at[h, d // 2],
                device_id=(lax.bitwise_xor(v, 1), p),
                device_id_type=MESH,
            )

        def to_core(self, d, h):
            copy = self.core_copy(d, h)
            copy.start()
            pending.append(copy)

        def begin(self):
            for h in range(2):
                self.to_chip(0, h, 0)
            for h in range(2):
                self.to_core(0, h)

        def second(self):
            for k in range(1, len(chips)):
                for h in range(2):
                    self.to_chip(0, h, k)

        def take(self, d, h, k):
            got = half(self.all.at[lax.bitwise_xor(v, d)], h)
            pltpu.make_async_remote_copy(
                src_ref=got, dst_ref=got, send_sem=self.send.at[0],
                recv_sem=self.recv.at[h, d // 2], device_id=(lax.bitwise_xor(v, 1), p),
                device_id_type=MESH,
            ).wait_recv()
            for later in range(k + 1, len(chips)):
                self.to_chip(d, h, later)
            self.to_core(d, h)

        def take_core(self, d):
            for h in range(2):
                got = half(self.all.at[lax.bitwise_xor(v, d ^ 1)], h)
                pltpu.make_async_remote_copy(
                    src_ref=got, dst_ref=got, send_sem=self.send.at[0],
                    recv_sem=self.core_recv.at[h, d // 2], device_id=(lax.bitwise_xor(v, 1), p),
                    device_id_type=MESH,
                ).wait_recv()

    gather_a = Gather(a_hbm, a_all, a_send, a_recv, a_core_send, a_core_recv)
    gather_b = Gather(None, b_all, b_send, b_recv, b_core_send, b_core_recv)

    def up_copy(c, i):
        return pltpu.make_async_remote_copy(
            src_ref=part.at[c, cut(i)], dst_ref=recv_up.at[c, cut(i)],
            send_sem=up_send.at[c, i], recv_sem=up_recv.at[c, i],
            device_id=(v, lax.rem(p + 1, K)), device_id_type=MESH,
        )

    def dn_copy(c, i):
        return pltpu.make_async_remote_copy(
            src_ref=part.at[c, cut(i)], dst_ref=recv_dn.at[c, cut(i)],
            send_sem=dn_send.at[c, i], recv_sem=dn_recv.at[c, i],
            device_id=(v, lax.rem(p + K - 1, K)), device_id_type=MESH,
        )

    running = jnp.int32(0)
    ends[0] = running
    for j in range(V * var_dev):
        running = running + counts_ref[v, j]
        ends[j + 1] = running

    def send_early(c, i):
        @pl.when(first & ((c > 2) | ((c == 2) & (i < PIECES - 1))))
        def _():
            up_copy(c, i).start()

        @pl.when(last & ((c < K - 3) | ((c == K - 3) & (i < PIECES - 1))))
        def _():
            dn_copy(c, i).start()

    send_early(chunk_at(0), 0)
    gather_a.begin()
    gather_a.second()

    @pl.loop(1, PIECES)
    def _(i):
        tok_copy(i).wait()
        base(chunk_at(0), i)
        send_early(chunk_at(0), i)

    @pl.loop(1, K)
    def _(k):
        c = chunk_at(k)
        w_copy(k).wait()

        @pl.loop(0, PIECES)
        def _(i):
            base(c, i)
            send_early(c, i)

    own_b.wait()
    for j in range(var_dev):
        turned = jnp.broadcast_to(scale_ref[j : j + 1, :].astype(jnp.float32), (R, R)).T
        for q in range(cols // R):
            at = pl.ds(q * R, R)
            b_all[v, j, :, at] = (b_raw[j, :, at].astype(jnp.float32) * turned).astype(jnp.bfloat16)

    def owner_mask(o, j, i, size, n):
        at = lax.broadcasted_iota(jnp.int32, (size, n), 0) + i * size
        return (at >= ends[o * var_dev + j]) & (at < ends[o * var_dev + j + 1])

    def rank_blocks(lo, hi, clear=False):
        @pl.loop(lo, hi)
        def _(d):
            o = lax.bitwise_xor(v, d)
            both = jnp.concatenate([a_all[o, j] for j in range(var_dev)], axis=1)
            product = jnp.dot(tok[...], both, preferred_element_type=jnp.float32)
            picked = rank[...]
            if clear:
                picked = jnp.where(d == lo, jnp.zeros_like(picked), picked)
            for j in range(var_dev):
                picked = jnp.where(owner_mask(o, j, 0, rows, R), product[:, j * R : (j + 1) * R], picked)
            rank[...] = picked

    def add_up(c, i):
        @pl.when((p > 0) & (p < c))
        def _():
            up_copy(c, i).wait_recv()
            part[c, cut(i)] = (
                part[c, cut(i)].astype(jnp.float32) + recv_up[c, cut(i)].astype(jnp.float32)
            ).astype(jnp.bfloat16)
            up_copy(c, i).start()

    def add_dn(c, i):
        @pl.when((p < K - 1) & (p > c))
        def _():
            dn_copy(c, i).wait_recv()
            part[c, cut(i)] = (
                part[c, cut(i)].astype(jnp.float32) + recv_dn[c, cut(i)].astype(jnp.float32)
            ).astype(jnp.bfloat16)
            dn_copy(c, i).start()

    def near(step, lo, hi):
        @pl.loop(lo, hi)
        def _(i):
            @pl.when(low_half)
            def _():
                add_up(K - 1 - step, i)

            @pl.when(jnp.logical_not(low_half))
            def _():
                add_dn(step, i)

    def far(step, lo, hi):
        @pl.loop(lo, hi)
        def _(i):
            @pl.when(low_half)
            def _():
                add_dn(step, i)

            @pl.when(jnp.logical_not(low_half))
            def _():
                add_up(K - 1 - step, i)

    direct, routed = [], []
    for k in range(len(chips)):
        for h in range(2):
            for t in span(orders[h][:k]):
                (direct if k == 0 else routed).append((orders[h][k] ^ t, h, k))
    more = K > 3
    near(0, 0, 2)
    for d, h, k in direct:
        gather_a.take(d, h, k)
    own_a.wait()
    gather_a.take_core(0)
    rank_blocks(0, 2, clear=True)
    near(0, 2, 3)
    far(0, 0, 1)
    near(0, 3, PIECES)
    for d, h, k in routed:
        if d in chips:
            gather_a.take(d, h, k)
    if len(chips) == 2:
        gather_a.take_core(2)
        gather_a.take_core(4)
        rank_blocks(2, 4)
        far(0, 1, 2)
        if more:
            near(1, 0, 1)
        rank_blocks(4, 6)
    far(0, 2, PIECES)
    if more:
        near(1, 1, 2)
    for d, h, k in routed:
        if d not in chips:
            gather_a.take(d, h, k)
    if len(chips) == 2:
        rank_blocks(6, 7)
        gather_a.take_core(6)
        rank_blocks(7, 8)
    else:
        for d in range(2, V, 2):
            gather_a.take_core(d)
        rank_blocks(2, V)

    def rup_copy(i):
        return pltpu.make_async_remote_copy(
            src_ref=rank_send_up.at[cut(i)], dst_ref=rank_up.at[cut(i)],
            send_sem=rup_send.at[i], recv_sem=rup_recv.at[i],
            device_id=(v, lax.rem(p + 1, K)), device_id_type=MESH,
        )

    def rdn_copy(i):
        return pltpu.make_async_remote_copy(
            src_ref=rank_send_dn.at[cut(i)], dst_ref=rank_dn.at[cut(i)],
            send_sem=rdn_send.at[i], recv_sem=rdn_recv.at[i],
            device_id=(v, lax.rem(p + K - 1, K)), device_id_type=MESH,
        )

    @pl.when(first)
    def _():
        rank_send_up[...] = rank[...].astype(jnp.bfloat16)
        for i in range(PIECES):
            rup_copy(i).start()

    @pl.when(last)
    def _():
        rank_send_dn[...] = rank[...].astype(jnp.bfloat16)
        for i in range(PIECES):
            rdn_copy(i).start()

    @pl.when(first)
    def _():
        up_copy(2, PIECES - 1).start()
        for i in range(PIECES):
            up_copy(1, i).start()

    @pl.when(last)
    def _():
        dn_copy(K - 3, PIECES - 1).start()
        for i in range(PIECES):
            dn_copy(K - 2, i).start()

    gather_b.begin()
    gather_b.second()
    if more:
        near(1, 2, 3)

    def rank_up_step(i):
        @pl.when(p > 0)
        def _():
            rup_copy(i).wait_recv()

            @pl.when(p < K - 1)
            def _():
                rank_send_up[cut(i)] = (
                    rank[cut(i)] + rank_up[cut(i)].astype(jnp.float32)
                ).astype(jnp.bfloat16)
                rup_copy(i).start()

    def rank_dn_step(i):
        @pl.when(p < K - 1)
        def _():
            rdn_copy(i).wait_recv()

            @pl.when(p > 0)
            def _():
                rank_send_dn[cut(i)] = (
                    rank[cut(i)] + rank_dn[cut(i)].astype(jnp.float32)
                ).astype(jnp.bfloat16)
                rdn_copy(i).start()

    def rank_turn(turn):
        @pl.loop(0, PIECES)
        def _(i):
            @pl.when(low_half if turn == 0 else jnp.logical_not(low_half))
            def _():
                rank_up_step(i)

            @pl.when(jnp.logical_not(low_half) if turn == 0 else low_half)
            def _():
                rank_dn_step(i)

    rank_turn(0)
    for d, h, k in direct:
        gather_b.take(d, h, k)
    rank_turn(1)
    if more:
        near(1, 3, PIECES)
        far(1, 0, PIECES)
    for step in range(2, K - 2):
        near(step, 0, PIECES)
        far(step, 0, PIECES)
    for d, h, k in routed:
        gather_b.take(d, h, k)
    for d in range(0, V, 2):
        gather_b.take_core(d)

    @pl.loop(0, PIECES)
    def _(i):
        @pl.when(p > 0)
        def _():
            rank[cut(i)] += rank_up[cut(i)].astype(jnp.float32)

        @pl.when(p < K - 1)
        def _():
            rank[cut(i)] += rank_dn[cut(i)].astype(jnp.float32)

        low = rank[cut(i)].astype(jnp.bfloat16)
        zero = jnp.zeros_like(low)
        wide = jnp.concatenate(
            [
                jnp.where(owner_mask(o, j, i, piece, R), low, zero)
                for o in range(V)
                for j in range(var_dev)
            ],
            axis=1,
        )
        delta = jnp.dot(
            wide, b_all[...].reshape(V * var_dev * R, cols), preferred_element_type=jnp.float32
        ).astype(jnp.bfloat16)
        total[cut(i)] = delta.astype(jnp.float32) + part[p, cut(i)].astype(jnp.float32)

    def last_up(i):
        @pl.when(p > 0)
        def _():
            up_copy(p, i).wait_recv()
            total[cut(i)] += recv_up[p, cut(i)].astype(jnp.float32)

    def last_dn(i):
        @pl.when(p < K - 1)
        def _():
            dn_copy(p, i).wait_recv()
            total[cut(i)] += recv_dn[p, cut(i)].astype(jnp.float32)

    @pl.loop(0, PIECES)
    def _(i):
        @pl.when(low_half)
        def _():
            last_dn(i)

        @pl.when(jnp.logical_not(low_half))
        def _():
            last_up(i)

    def out_copy(i):
        return pltpu.make_async_copy(outv.at[cut(i)], out_hbm.at[cut(i)], out_sem.at[i])

    @pl.loop(0, PIECES)
    def _(i):
        @pl.when(low_half)
        def _():
            last_up(i)

        @pl.when(jnp.logical_not(low_half))
        def _():
            last_dn(i)

        outv[cut(i)] = total[cut(i)].astype(jnp.bfloat16)
        out_copy(i).start()

    for copy in pending:
        copy.wait_send()

    @pl.loop(0, PIECES)
    def _(i):
        for c in range(K):
            @pl.when(p < c)
            def _():
                up_copy(c, i).wait_send()

            @pl.when(p > c)
            def _():
                dn_copy(c, i).wait_send()

        @pl.when(p < K - 1)
        def _():
            rup_copy(i).wait_send()

        @pl.when(p > 0)
        def _():
            rdn_copy(i).wait_send()

        out_copy(i).wait()


def body(V, K, tokens, kv_weight, factor_a, factor_scale, factor_b, counts):
    rows, feats = tokens.shape
    wide = kv_weight.shape[1]
    cols = wide // K
    var_dev, _, R = factor_a.shape
    DMA = pltpu.SemaphoreType.DMA
    bf16, f32 = jnp.bfloat16, jnp.float32
    anywhere = pl.BlockSpec(memory_space=pl.ANY)
    sends = 2 * (V // 2 - 1)
    halves = (2, V // 2)
    gather_sems = [DMA((sends,)), DMA(halves), DMA(halves), DMA(halves)]
    chain = [DMA((K, PIECES)), DMA((K, PIECES))]
    rank_chain = [DMA((PIECES,)), DMA((PIECES,))]
    return pl.pallas_call(
        functools.partial(kernel, V, K),
        out_shape=jax.ShapeDtypeStruct((rows, cols), bf16),
        in_specs=[
            anywhere, anywhere, anywhere,
            pl.BlockSpec(memory_space=pltpu.VMEM),
            anywhere,
            pl.BlockSpec(memory_space=pltpu.SMEM),
        ],
        out_specs=anywhere,
        scratch_shapes=[
            pltpu.VMEM((rows, feats), bf16),
            pltpu.VMEM((K, feats, cols), bf16),
            pltpu.VMEM((V, var_dev, feats, R), bf16),
            pltpu.VMEM((var_dev, R, cols), bf16),
            pltpu.VMEM((V, var_dev, R, cols), bf16),
            pltpu.VMEM((K, rows, cols), bf16),
            pltpu.VMEM((K, rows, cols), bf16),
            pltpu.VMEM((K, rows, cols), bf16),
            pltpu.VMEM((rows, R), f32),
            pltpu.VMEM((rows, R), bf16),
            pltpu.VMEM((rows, R), bf16),
            pltpu.VMEM((rows, R), bf16),
            pltpu.VMEM((rows, R), bf16),
            pltpu.VMEM((rows, cols), f32),
            pltpu.VMEM((rows, cols), bf16),
            pltpu.SMEM((V * var_dev + 1,), jnp.int32),
            DMA((PIECES,)), DMA((K,)), DMA((2,)), DMA((PIECES,)),
            *gather_sems, *gather_sems, *chain, *chain, *rank_chain, *rank_chain,
        ],
        compiler_params=pltpu.CompilerParams(
            collective_id=0, has_side_effects=True, vmem_limit_bytes=60 << 20
        ),
    )(tokens, kv_weight, factor_a, factor_scale, factor_b, counts)


def solution(mesh):
    return jax.shard_map(
        functools.partial(body, mesh.shape["var"], mesh.shape["tp"]),
        mesh=mesh,
        in_specs=(
            P("var", "tp"),
            P("tp", None),
            P("var", "tp", None),
            P("var", None),
            P("var", None, "tp"),
            P(),
        ),
        out_specs=P("var", "tp"),
        check_vma=False,
    )
```

```python
import functools

import jax
import jax.numpy as jnp
from jax import lax
from jax.experimental import pallas as pl
from jax.experimental.pallas import tpu as pltpu
from jax.sharding import PartitionSpec as P

MESH = pl.DeviceIdType.MESH
PIECES = 4
SUBS = 2


def span(masks):
    found = [0]
    for mask in masks:
        found = found + [old ^ mask for old in found]
    return found


def kernel(
    V, K,
    tok_hbm, w_hbm, a_hbm, scale_ref, b_hbm, counts_ref,
    out,
    tok, w, a_all, b_raw, b_all, part, recv_up, recv_dn, rank, rank_up, rank_dn, rank_send_up,
    rank_send_dn, total, ends,
    tok_sem, w_sem, own_sem,
    a_send, a_recv, a_core_send, a_core_recv, b_send, b_recv, b_core_send, b_core_recv,
    up_send, up_recv, dn_send, dn_recv, rup_send, rup_recv, rdn_send, rdn_recv,
):
    v = lax.axis_index("var")
    p = lax.axis_index("tp")
    rows, feats = tok.shape
    cols = w.shape[2]
    var_dev = a_all.shape[1]
    R = a_all.shape[3]
    piece = rows // PIECES
    first, last = p == 0, p == K - 1
    low_half = p < K // 2

    def cut(i):
        return pl.ds(pl.multiple_of(i * piece, piece), piece)

    def chunk_at(k):
        c = k // 2
        c = jnp.where(k % 2 == 0, K - 1 - c, c)
        return jnp.where(low_half, c, K - 1 - c)

    def tok_copy(i):
        return pltpu.make_async_copy(tok_hbm.at[cut(i)], tok.at[cut(i)], tok_sem.at[i])

    def w_copy(k):
        c = chunk_at(k)
        return pltpu.make_async_copy(
            w_hbm.at[:, pl.ds(pl.multiple_of(c * cols, cols), cols)], w.at[c], w_sem.at[k]
        )

    w_copy(0).start()
    tok_copy(0).start()
    own_a = pltpu.make_async_copy(a_hbm, a_all.at[v], own_sem.at[0])
    own_b = pltpu.make_async_copy(b_hbm, b_raw, own_sem.at[1])

    masks = []
    m = 1
    while m < V:
        masks.append(m)
        m *= 2
    barrier = pltpu.get_barrier_semaphore()
    for m in masks:
        pl.semaphore_signal(barrier, inc=1, device_id=(lax.bitwise_xor(v, m), p), device_id_type=MESH)

    @pl.when(p > 0)
    def _():
        pl.semaphore_signal(barrier, inc=1, device_id=(v, p - 1), device_id_type=MESH)

    @pl.when(p < K - 1)
    def _():
        pl.semaphore_signal(barrier, inc=1, device_id=(v, p + 1), device_id_type=MESH)

    def base(c, i):
        part[c, cut(i)] = jnp.dot(
            tok[cut(i)], w[c], preferred_element_type=jnp.float32
        ).astype(jnp.bfloat16)

    tok_copy(0).wait()
    w_copy(0).wait()
    for i in range(1, PIECES):
        tok_copy(i).start()
    for k in range(1, K):
        w_copy(k).start()
    own_a.start()
    own_b.start()

    pl.semaphore_wait(
        barrier, len(masks) + (p > 0).astype(jnp.int32) + (p < K - 1).astype(jnp.int32)
    )

    chips = masks[1:]
    orders = (chips, chips[::-1])

    def half(ref, h):
        size = ref.shape[1] // 2
        return ref.at[:, pl.ds(h * size, size)]

    pending = []

    class Gather:
        def __init__(self, own, everything, send, recv, core_send, core_recv):
            self.own, self.all = own, everything
            self.send, self.recv, self.core_send, self.core_recv = send, recv, core_send, core_recv
            self.used = 0

        def block(self, d, h):
            if d == 0 and self.own is not None:
                return half(self.own, h)
            return half(self.all.at[lax.bitwise_xor(v, d)], h)

        def to_chip(self, d, h, k):
            m = orders[h][k]
            copy = pltpu.make_async_remote_copy(
                src_ref=self.block(d, h),
                dst_ref=half(self.all.at[lax.bitwise_xor(v, d)], h),
                send_sem=self.send.at[self.used],
                recv_sem=self.recv.at[h, (d ^ m) // 2],
                device_id=(lax.bitwise_xor(v, m), p),
                device_id_type=MESH,
            )
            self.used += 1
            copy.start()
            pending.append(copy)

        def core_copy(self, d, h):
            return pltpu.make_async_remote_copy(
                src_ref=self.block(d, h),
                dst_ref=half(self.all.at[lax.bitwise_xor(v, d)], h),
                send_sem=self.core_send.at[h, d // 2],
                recv_sem=self.core_recv.at[h, d // 2],
                device_id=(lax.bitwise_xor(v, 1), p),
                device_id_type=MESH,
            )

        def to_core(self, d, h):
            copy = self.core_copy(d, h)
            copy.start()
            pending.append(copy)

        def begin(self):
            for h in range(2):
                self.to_chip(0, h, 0)
            for h in range(2):
                self.to_core(0, h)

        def second(self):
            for k in range(1, len(chips)):
                for h in range(2):
                    self.to_chip(0, h, k)

        def take(self, d, h, k):
            got = half(self.all.at[lax.bitwise_xor(v, d)], h)
            pltpu.make_async_remote_copy(
                src_ref=got, dst_ref=got, send_sem=self.send.at[0],
                recv_sem=self.recv.at[h, d // 2], device_id=(lax.bitwise_xor(v, 1), p),
                device_id_type=MESH,
            ).wait_recv()
            for later in range(k + 1, len(chips)):
                self.to_chip(d, h, later)
            self.to_core(d, h)

        def take_core(self, d):
            for h in range(2):
                got = half(self.all.at[lax.bitwise_xor(v, d ^ 1)], h)
                pltpu.make_async_remote_copy(
                    src_ref=got, dst_ref=got, send_sem=self.send.at[0],
                    recv_sem=self.core_recv.at[h, d // 2], device_id=(lax.bitwise_xor(v, 1), p),
                    device_id_type=MESH,
                ).wait_recv()

    gather_a = Gather(a_hbm, a_all, a_send, a_recv, a_core_send, a_core_recv)
    gather_b = Gather(None, b_all, b_send, b_recv, b_core_send, b_core_recv)

    def chain_copy(src, dst, send, recv, c, i, here, to):
        return pltpu.make_async_remote_copy(
            src_ref=src.at[c, here], dst_ref=dst.at[c, here],
            send_sem=send.at[c, i], recv_sem=recv.at[c, i],
            device_id=(v, to), device_id_type=MESH,
        )

    def up_copy(c, i):
        return pltpu.make_async_remote_copy(
            src_ref=part.at[c, cut(i)], dst_ref=recv_up.at[c, cut(i)],
            send_sem=up_send.at[c, i], recv_sem=up_recv.at[c, i],
            device_id=(v, lax.rem(p + 1, K)), device_id_type=MESH,
        )

    def dn_copy(c, i):
        return pltpu.make_async_remote_copy(
            src_ref=part.at[c, cut(i)], dst_ref=recv_dn.at[c, cut(i)],
            send_sem=dn_send.at[c, i], recv_sem=dn_recv.at[c, i],
            device_id=(v, lax.rem(p + K - 1, K)), device_id_type=MESH,
        )

    running = jnp.int32(0)
    ends[0] = running
    for j in range(V * var_dev):
        running = running + counts_ref[v, j]
        ends[j + 1] = running

    def send_early(c, i):
        @pl.when(first & (c >= 2))
        def _():
            up_copy(c, i).start()

        @pl.when(last & (c <= K - 3))
        def _():
            dn_copy(c, i).start()

    sub = piece // SUBS

    @pl.loop(0, SUBS)
    def _(i):
        here = pl.ds(pl.multiple_of(i * sub, sub), sub)
        c = chunk_at(0)
        part[c, here] = jnp.dot(
            tok[here], w[c], preferred_element_type=jnp.float32
        ).astype(jnp.bfloat16)

        @pl.when(first)
        def _():
            chain_copy(part, recv_up, up_send, up_recv, c, 0, here, lax.rem(p + 1, K)).start()

        @pl.when(last)
        def _():
            chain_copy(part, recv_dn, dn_send, dn_recv, c, 0, here, lax.rem(p + K - 1, K)).start()

    gather_a.begin()
    gather_a.second()

    @pl.loop(1, PIECES)
    def _(i):
        tok_copy(i).wait()
        base(chunk_at(0), i)
        send_early(chunk_at(0), i)

    @pl.loop(1, K)
    def _(k):
        c = chunk_at(k)
        w_copy(k).wait()

        @pl.loop(0, PIECES)
        def _(i):
            base(c, i)
            send_early(c, i)

    own_b.wait()
    for j in range(var_dev):
        turned = jnp.broadcast_to(scale_ref[j : j + 1, :].astype(jnp.float32), (R, R)).T
        for q in range(cols // R):
            at = pl.ds(q * R, R)
            b_all[v, j, :, at] = (b_raw[j, :, at].astype(jnp.float32) * turned).astype(jnp.bfloat16)

    def owner_mask(o, j, i, size, n):
        at = lax.broadcasted_iota(jnp.int32, (size, n), 0) + i * size
        return (at >= ends[o * var_dev + j]) & (at < ends[o * var_dev + j + 1])

    def rank_blocks(lo, hi, clear=False):
        @pl.loop(lo, hi)
        def _(d):
            o = lax.bitwise_xor(v, d)
            both = jnp.concatenate([a_all[o, j] for j in range(var_dev)], axis=1)
            product = jnp.dot(tok[...], both, preferred_element_type=jnp.float32)
            picked = rank[...]
            if clear:
                picked = jnp.where(d == lo, jnp.zeros_like(picked), picked)
            for j in range(var_dev):
                picked = jnp.where(owner_mask(o, j, 0, rows, R), product[:, j * R : (j + 1) * R], picked)
            rank[...] = picked

    def add_up(c, i):
        @pl.when((p > 0) & (p < c))
        def _():
            up_copy(c, i).wait_recv()
            part[c, cut(i)] = (
                part[c, cut(i)].astype(jnp.float32) + recv_up[c, cut(i)].astype(jnp.float32)
            ).astype(jnp.bfloat16)
            up_copy(c, i).start()

    def add_dn(c, i):
        @pl.when((p < K - 1) & (p > c))
        def _():
            dn_copy(c, i).wait_recv()
            part[c, cut(i)] = (
                part[c, cut(i)].astype(jnp.float32) + recv_dn[c, cut(i)].astype(jnp.float32)
            ).astype(jnp.bfloat16)
            dn_copy(c, i).start()

    def near(step, lo, hi):
        @pl.loop(lo, hi)
        def _(i):
            @pl.when(low_half)
            def _():
                add_up(K - 1 - step, i)

            @pl.when(jnp.logical_not(low_half))
            def _():
                add_dn(step, i)

    def far(step, lo, hi):
        @pl.loop(lo, hi)
        def _(i):
            @pl.when(low_half)
            def _():
                add_dn(step, i)

            @pl.when(jnp.logical_not(low_half))
            def _():
                add_up(K - 1 - step, i)

    direct, routed = [], []
    for k in range(len(chips)):
        for h in range(2):
            for t in span(orders[h][:k]):
                (direct if k == 0 else routed).append((orders[h][k] ^ t, h, k))
    more = K > 3
    near(0, 0, 2)
    for d, h, k in direct:
        gather_a.take(d, h, k)
    own_a.wait()
    gather_a.take_core(0)
    rank_blocks(0, 2, clear=True)
    near(0, 2, 3)
    far(0, 0, 1)
    near(0, 3, PIECES)
    for d, h, k in routed:
        if d in chips:
            gather_a.take(d, h, k)
    if len(chips) == 2:
        gather_a.take_core(2)
        gather_a.take_core(4)
        rank_blocks(2, 4)
        far(0, 1, 2)
        if more:
            near(1, 0, 1)
        rank_blocks(4, 6)
    far(0, 2, PIECES)
    if more:
        near(1, 1, 2)
    for d, h, k in routed:
        if d not in chips:
            gather_a.take(d, h, k)
    if len(chips) == 2:
        rank_blocks(6, 7)
        gather_a.take_core(6)
        rank_blocks(7, 8)
    else:
        for d in range(2, V, 2):
            gather_a.take_core(d)
        rank_blocks(2, V)

    def rup_copy(i):
        return pltpu.make_async_remote_copy(
            src_ref=rank_send_up.at[cut(i)], dst_ref=rank_up.at[cut(i)],
            send_sem=rup_send.at[i], recv_sem=rup_recv.at[i],
            device_id=(v, lax.rem(p + 1, K)), device_id_type=MESH,
        )

    def rdn_copy(i):
        return pltpu.make_async_remote_copy(
            src_ref=rank_send_dn.at[cut(i)], dst_ref=rank_dn.at[cut(i)],
            send_sem=rdn_send.at[i], recv_sem=rdn_recv.at[i],
            device_id=(v, lax.rem(p + K - 1, K)), device_id_type=MESH,
        )

    @pl.when(first)
    def _():
        rank_send_up[...] = rank[...].astype(jnp.bfloat16)
        for i in range(PIECES):
            rup_copy(i).start()

    @pl.when(last)
    def _():
        rank_send_dn[...] = rank[...].astype(jnp.bfloat16)
        for i in range(PIECES):
            rdn_copy(i).start()

    @pl.when(first)
    def _():
        for i in range(PIECES):
            up_copy(1, i).start()

    @pl.when(last)
    def _():
        for i in range(PIECES):
            dn_copy(K - 2, i).start()

    gather_b.begin()
    gather_b.second()
    if more:
        near(1, 2, 3)

    def rank_up_step(i):
        @pl.when(p > 0)
        def _():
            rup_copy(i).wait_recv()

            @pl.when(p < K - 1)
            def _():
                rank_send_up[cut(i)] = (
                    rank[cut(i)] + rank_up[cut(i)].astype(jnp.float32)
                ).astype(jnp.bfloat16)
                rup_copy(i).start()

    def rank_dn_step(i):
        @pl.when(p < K - 1)
        def _():
            rdn_copy(i).wait_recv()

            @pl.when(p > 0)
            def _():
                rank_send_dn[cut(i)] = (
                    rank[cut(i)] + rank_dn[cut(i)].astype(jnp.float32)
                ).astype(jnp.bfloat16)
                rdn_copy(i).start()

    def rank_turn(turn):
        @pl.loop(0, PIECES)
        def _(i):
            @pl.when(low_half if turn == 0 else jnp.logical_not(low_half))
            def _():
                rank_up_step(i)

            @pl.when(jnp.logical_not(low_half) if turn == 0 else low_half)
            def _():
                rank_dn_step(i)

    rank_turn(0)
    for d, h, k in direct:
        gather_b.take(d, h, k)
    rank_turn(1)
    if more:
        near(1, 3, PIECES)
        far(1, 0, PIECES)
    for step in range(2, K - 2):
        near(step, 0, PIECES)
        far(step, 0, PIECES)
    for d, h, k in routed:
        gather_b.take(d, h, k)
    for d in range(0, V, 2):
        gather_b.take_core(d)

    @pl.loop(0, PIECES)
    def _(i):
        @pl.when(p > 0)
        def _():
            rank[cut(i)] += rank_up[cut(i)].astype(jnp.float32)

        @pl.when(p < K - 1)
        def _():
            rank[cut(i)] += rank_dn[cut(i)].astype(jnp.float32)

        low = rank[cut(i)].astype(jnp.bfloat16)
        zero = jnp.zeros_like(low)
        wide = jnp.concatenate(
            [
                jnp.where(owner_mask(o, j, i, piece, R), low, zero)
                for o in range(V)
                for j in range(var_dev)
            ],
            axis=1,
        )
        delta = jnp.dot(
            wide, b_all[...].reshape(V * var_dev * R, cols), preferred_element_type=jnp.float32
        ).astype(jnp.bfloat16)
        total[cut(i)] = delta.astype(jnp.float32) + part[p, cut(i)].astype(jnp.float32)

    def last_up(i):
        @pl.when(p > 0)
        def _():
            up_copy(p, i).wait_recv()
            total[cut(i)] += recv_up[p, cut(i)].astype(jnp.float32)

    def last_dn(i):
        @pl.when(p < K - 1)
        def _():
            dn_copy(p, i).wait_recv()
            total[cut(i)] += recv_dn[p, cut(i)].astype(jnp.float32)

    @pl.loop(0, PIECES)
    def _(i):
        @pl.when(low_half)
        def _():
            last_dn(i)

        @pl.when(jnp.logical_not(low_half))
        def _():
            last_up(i)

    @pl.loop(0, PIECES)
    def _(i):
        @pl.when(low_half)
        def _():
            last_up(i)

        @pl.when(jnp.logical_not(low_half))
        def _():
            last_dn(i)

        out[cut(i)] = total[cut(i)].astype(jnp.bfloat16)

    for copy in pending:
        copy.wait_send()

    @pl.loop(0, PIECES)
    def _(i):
        for c in range(K):
            @pl.when(p < c)
            def _():
                up_copy(c, i).wait_send()

            @pl.when(p > c)
            def _():
                dn_copy(c, i).wait_send()

        @pl.when(p < K - 1)
        def _():
            rup_copy(i).wait_send()

        @pl.when(p > 0)
        def _():
            rdn_copy(i).wait_send()


def body(V, K, tokens, kv_weight, factor_a, factor_scale, factor_b, counts):
    rows, feats = tokens.shape
    wide = kv_weight.shape[1]
    cols = wide // K
    var_dev, _, R = factor_a.shape
    DMA = pltpu.SemaphoreType.DMA
    bf16, f32 = jnp.bfloat16, jnp.float32
    anywhere = pl.BlockSpec(memory_space=pl.ANY)
    sends = 2 * (V // 2 - 1)
    halves = (2, V // 2)
    gather_sems = [DMA((sends,)), DMA(halves), DMA(halves), DMA(halves)]
    chain = [DMA((K, PIECES)), DMA((K, PIECES))]
    rank_chain = [DMA((PIECES,)), DMA((PIECES,))]
    return pl.pallas_call(
        functools.partial(kernel, V, K),
        out_shape=pltpu.VMEM((rows, cols), bf16),
        in_specs=[
            anywhere, anywhere, anywhere,
            pl.BlockSpec(memory_space=pltpu.VMEM),
            anywhere,
            pl.BlockSpec(memory_space=pltpu.SMEM),
        ],
        out_specs=pl.BlockSpec(memory_space=pltpu.VMEM),
        scratch_shapes=[
            pltpu.VMEM((rows, feats), bf16),
            pltpu.VMEM((K, feats, cols), bf16),
            pltpu.VMEM((V, var_dev, feats, R), bf16),
            pltpu.VMEM((var_dev, R, cols), bf16),
            pltpu.VMEM((V, var_dev, R, cols), bf16),
            pltpu.VMEM((K, rows, cols), bf16),
            pltpu.VMEM((K, rows, cols), bf16),
            pltpu.VMEM((K, rows, cols), bf16),
            pltpu.VMEM((rows, R), f32),
            pltpu.VMEM((rows, R), bf16),
            pltpu.VMEM((rows, R), bf16),
            pltpu.VMEM((rows, R), bf16),
            pltpu.VMEM((rows, R), bf16),
            pltpu.VMEM((rows, cols), f32),
            pltpu.SMEM((V * var_dev + 1,), jnp.int32),
            DMA((PIECES,)), DMA((K,)), DMA((2,)),
            *gather_sems, *gather_sems, *chain, *chain, *rank_chain, *rank_chain,
        ],
        compiler_params=pltpu.CompilerParams(
            collective_id=0, has_side_effects=True, vmem_limit_bytes=60 << 20
        ),
    )(tokens, kv_weight, factor_a, factor_scale, factor_b, counts)


def solution(mesh):
    return jax.shard_map(
        functools.partial(body, mesh.shape["var"], mesh.shape["tp"]),
        mesh=mesh,
        in_specs=(
            P("var", "tp"),
            P("tp", None),
            P("var", "tp", None),
            P("var", None),
            P("var", None, "tp"),
            P(),
        ),
        out_specs=P("var", "tp"),
        check_vma=False,
    )
```

```python
import functools

import jax
import jax.numpy as jnp
from jax import lax
from jax.experimental import pallas as pl
from jax.experimental.pallas import tpu as pltpu
from jax.sharding import PartitionSpec as P

MESH = pl.DeviceIdType.MESH
PIECES = 4
SUBS = 2


def span(masks):
    found = [0]
    for mask in masks:
        found = found + [old ^ mask for old in found]
    return found


def kernel(
    V, K,
    tok_hbm, w_hbm, a_hbm, scale_hbm, b_hbm, counts_hbm,
    out,
    tok, w, a_all, b_raw, b_all, part, recv_up, recv_dn, rank, rank_up, rank_dn, rank_send_up,
    rank_send_dn, total, scale_ref, counts_ref, ends,
    tok_sem, w_sem, own_sem,
    a_send, a_recv, a_core_send, a_core_recv, b_send, b_recv, b_core_send, b_core_recv,
    up_send, up_recv, dn_send, dn_recv, rup_send, rup_recv, rdn_send, rdn_recv,
):
    v = lax.axis_index("var")
    p = lax.axis_index("tp")
    rows, feats = tok.shape
    cols = w.shape[2]
    var_dev = a_all.shape[1]
    R = a_all.shape[3]
    piece = rows // PIECES
    first, last = p == 0, p == K - 1
    low_half = p < K // 2

    def cut(i):
        return pl.ds(pl.multiple_of(i * piece, piece), piece)

    def chunk_at(k):
        c = k // 2
        c = jnp.where(k % 2 == 0, K - 1 - c, c)
        return jnp.where(low_half, c, K - 1 - c)

    def tok_copy(i):
        return pltpu.make_async_copy(tok_hbm.at[cut(i)], tok.at[cut(i)], tok_sem.at[i])

    def w_copy(k):
        c = chunk_at(k)
        return pltpu.make_async_copy(
            w_hbm.at[:, pl.ds(pl.multiple_of(c * cols, cols), cols)], w.at[c], w_sem.at[k]
        )

    half_cols = cols // 2

    def w_half(h):
        at = pl.multiple_of(chunk_at(0) * cols + h * half_cols, half_cols)
        return pltpu.make_async_copy(
            w_hbm.at[:, pl.ds(at, half_cols)],
            w.at[chunk_at(0), :, pl.ds(h * half_cols, half_cols)],
            w_sem.at[0 if h == 0 else K],
        )

    sub = piece // SUBS

    def tok_sub(i):
        here = pl.ds(i * sub, sub)
        return pltpu.make_async_copy(tok_hbm.at[here], tok.at[here], tok_sem.at[0 if i == 0 else PIECES])

    w_half(0).start()
    tok_sub(0).start()
    tok_sub(1).start()
    w_half(1).start()
    own_a = pltpu.make_async_copy(a_hbm, a_all.at[v], own_sem.at[0])
    own_b = pltpu.make_async_copy(b_hbm, b_raw, own_sem.at[1])
    own_scale = pltpu.make_async_copy(scale_hbm, scale_ref, own_sem.at[2])
    own_counts = pltpu.make_async_copy(counts_hbm, counts_ref, own_sem.at[3])

    masks = []
    m = 1
    while m < V:
        masks.append(m)
        m *= 2
    barrier = pltpu.get_barrier_semaphore()
    for m in masks:
        pl.semaphore_signal(barrier, inc=1, device_id=(lax.bitwise_xor(v, m), p), device_id_type=MESH)

    @pl.when(p > 0)
    def _():
        pl.semaphore_signal(barrier, inc=1, device_id=(v, p - 1), device_id_type=MESH)

    @pl.when(p < K - 1)
    def _():
        pl.semaphore_signal(barrier, inc=1, device_id=(v, p + 1), device_id_type=MESH)

    def base(c, i):
        part[c, cut(i)] = jnp.dot(
            tok[cut(i)], w[c], preferred_element_type=jnp.float32
        ).astype(jnp.bfloat16)

    tok_sub(0).wait()
    w_half(0).wait()
    for i in range(1, PIECES):
        tok_copy(i).start()
    for k in range(1, K):
        w_copy(k).start()
    own_counts.start()
    own_scale.start()
    own_a.start()
    own_b.start()

    pl.semaphore_wait(
        barrier, len(masks) + (p > 0).astype(jnp.int32) + (p < K - 1).astype(jnp.int32)
    )

    chips = masks[1:]
    orders = (chips, chips[::-1])

    def half(ref, h):
        size = ref.shape[1] // 2
        return ref.at[:, pl.ds(h * size, size)]

    pending = []

    class Gather:
        def __init__(self, own, everything, send, recv, core_send, core_recv):
            self.own, self.all = own, everything
            self.send, self.recv, self.core_send, self.core_recv = send, recv, core_send, core_recv
            self.used = 0

        def block(self, d, h):
            if d == 0 and self.own is not None:
                return half(self.own, h)
            return half(self.all.at[lax.bitwise_xor(v, d)], h)

        def to_chip(self, d, h, k):
            m = orders[h][k]
            copy = pltpu.make_async_remote_copy(
                src_ref=self.block(d, h),
                dst_ref=half(self.all.at[lax.bitwise_xor(v, d)], h),
                send_sem=self.send.at[self.used],
                recv_sem=self.recv.at[h, (d ^ m) // 2],
                device_id=(lax.bitwise_xor(v, m), p),
                device_id_type=MESH,
            )
            self.used += 1
            copy.start()
            pending.append(copy)

        def core_copy(self, d, h):
            return pltpu.make_async_remote_copy(
                src_ref=self.block(d, h),
                dst_ref=half(self.all.at[lax.bitwise_xor(v, d)], h),
                send_sem=self.core_send.at[h, d // 2],
                recv_sem=self.core_recv.at[h, d // 2],
                device_id=(lax.bitwise_xor(v, 1), p),
                device_id_type=MESH,
            )

        def to_core(self, d, h):
            copy = self.core_copy(d, h)
            copy.start()
            pending.append(copy)

        def begin(self):
            for h in range(2):
                self.to_chip(0, h, 0)
            for h in range(2):
                self.to_core(0, h)

        def second(self):
            for k in range(1, len(chips)):
                for h in range(2):
                    self.to_chip(0, h, k)

        def take(self, d, h, k):
            got = half(self.all.at[lax.bitwise_xor(v, d)], h)
            pltpu.make_async_remote_copy(
                src_ref=got, dst_ref=got, send_sem=self.send.at[0],
                recv_sem=self.recv.at[h, d // 2], device_id=(lax.bitwise_xor(v, 1), p),
                device_id_type=MESH,
            ).wait_recv()
            for later in range(k + 1, len(chips)):
                self.to_chip(d, h, later)
            self.to_core(d, h)

        def take_core(self, d):
            for h in range(2):
                got = half(self.all.at[lax.bitwise_xor(v, d ^ 1)], h)
                pltpu.make_async_remote_copy(
                    src_ref=got, dst_ref=got, send_sem=self.send.at[0],
                    recv_sem=self.core_recv.at[h, d // 2], device_id=(lax.bitwise_xor(v, 1), p),
                    device_id_type=MESH,
                ).wait_recv()

    gather_a = Gather(a_hbm, a_all, a_send, a_recv, a_core_send, a_core_recv)
    gather_b = Gather(None, b_all, b_send, b_recv, b_core_send, b_core_recv)

    def chain_copy(src, dst, send, recv, c, here, there, to):
        return pltpu.make_async_remote_copy(
            src_ref=src.at[c, here, there], dst_ref=dst.at[c, here, there],
            send_sem=send.at[c, 0], recv_sem=recv.at[c, 0],
            device_id=(v, to), device_id_type=MESH,
        )

    def up_copy(c, i):
        return pltpu.make_async_remote_copy(
            src_ref=part.at[c, cut(i)], dst_ref=recv_up.at[c, cut(i)],
            send_sem=up_send.at[c, i], recv_sem=up_recv.at[c, i],
            device_id=(v, lax.rem(p + 1, K)), device_id_type=MESH,
        )

    def dn_copy(c, i):
        return pltpu.make_async_remote_copy(
            src_ref=part.at[c, cut(i)], dst_ref=recv_dn.at[c, cut(i)],
            send_sem=dn_send.at[c, i], recv_sem=dn_recv.at[c, i],
            device_id=(v, lax.rem(p + K - 1, K)), device_id_type=MESH,
        )

    def send_early(c, i):
        @pl.when(first & (c >= 2))
        def _():
            up_copy(c, i).start()

        @pl.when(last & (c <= K - 3))
        def _():
            dn_copy(c, i).start()

    def opening(here, h):
        c = chunk_at(0)
        there = pl.ds(h * half_cols, half_cols)
        part[c, here, there] = jnp.dot(
            tok[here], w[c, :, there], preferred_element_type=jnp.float32
        ).astype(jnp.bfloat16)

        @pl.when(first)
        def _():
            chain_copy(part, recv_up, up_send, up_recv, c, here, there, lax.rem(p + 1, K)).start()

        @pl.when(last)
        def _():
            chain_copy(part, recv_dn, dn_send, dn_recv, c, here, there, lax.rem(p + K - 1, K)).start()

    opening(pl.ds(0, sub), 0)
    tok_sub(1).wait()
    opening(pl.ds(sub, sub), 0)
    w_half(1).wait()
    opening(pl.ds(0, piece), 1)
    gather_a.begin()
    gather_a.second()

    @pl.loop(1, PIECES)
    def _(i):
        tok_copy(i).wait()
        base(chunk_at(0), i)
        send_early(chunk_at(0), i)

    @pl.loop(1, K)
    def _(k):
        c = chunk_at(k)
        w_copy(k).wait()

        @pl.loop(0, PIECES)
        def _(i):
            base(c, i)
            send_early(c, i)

    own_counts.wait()
    running = jnp.int32(0)
    ends[0] = running
    for j in range(V * var_dev):
        running = running + counts_ref[v, j]
        ends[j + 1] = running

    own_b.wait()
    own_scale.wait()
    for j in range(var_dev):
        turned = jnp.broadcast_to(scale_ref[j : j + 1, :].astype(jnp.float32), (R, R)).T
        for q in range(cols // R):
            at = pl.ds(q * R, R)
            b_all[v, j, :, at] = (b_raw[j, :, at].astype(jnp.float32) * turned).astype(jnp.bfloat16)

    def owner_mask(o, j, i, size, n):
        at = lax.broadcasted_iota(jnp.int32, (size, n), 0) + i * size
        return (at >= ends[o * var_dev + j]) & (at < ends[o * var_dev + j + 1])

    def rank_blocks(lo, hi, clear=False):
        @pl.loop(lo, hi)
        def _(d):
            o = lax.bitwise_xor(v, d)
            both = jnp.concatenate([a_all[o, j] for j in range(var_dev)], axis=1)
            product = jnp.dot(tok[...], both, preferred_element_type=jnp.float32)
            picked = rank[...]
            if clear:
                picked = jnp.where(d == lo, jnp.zeros_like(picked), picked)
            for j in range(var_dev):
                picked = jnp.where(owner_mask(o, j, 0, rows, R), product[:, j * R : (j + 1) * R], picked)
            rank[...] = picked

    def add_up(c, i):
        @pl.when((p > 0) & (p < c))
        def _():
            up_copy(c, i).wait_recv()
            part[c, cut(i)] = (
                part[c, cut(i)].astype(jnp.float32) + recv_up[c, cut(i)].astype(jnp.float32)
            ).astype(jnp.bfloat16)
            up_copy(c, i).start()

    def add_dn(c, i):
        @pl.when((p < K - 1) & (p > c))
        def _():
            dn_copy(c, i).wait_recv()
            part[c, cut(i)] = (
                part[c, cut(i)].astype(jnp.float32) + recv_dn[c, cut(i)].astype(jnp.float32)
            ).astype(jnp.bfloat16)
            dn_copy(c, i).start()

    def near(step, lo, hi):
        @pl.loop(lo, hi)
        def _(i):
            @pl.when(low_half)
            def _():
                add_up(K - 1 - step, i)

            @pl.when(jnp.logical_not(low_half))
            def _():
                add_dn(step, i)

    def far(step, lo, hi):
        @pl.loop(lo, hi)
        def _(i):
            @pl.when(low_half)
            def _():
                add_dn(step, i)

            @pl.when(jnp.logical_not(low_half))
            def _():
                add_up(K - 1 - step, i)

    direct, routed = [], []
    for k in range(len(chips)):
        for h in range(2):
            for t in span(orders[h][:k]):
                (direct if k == 0 else routed).append((orders[h][k] ^ t, h, k))
    more = K > 3
    near(0, 0, 2)
    for d, h, k in direct:
        gather_a.take(d, h, k)
    own_a.wait()
    gather_a.take_core(0)
    rank_blocks(0, 2, clear=True)
    near(0, 2, 3)
    far(0, 0, 1)
    near(0, 3, PIECES)
    for d, h, k in routed:
        if d in chips:
            gather_a.take(d, h, k)
    if len(chips) == 2:
        gather_a.take_core(2)
        gather_a.take_core(4)
        rank_blocks(2, 4)
        far(0, 1, 2)
        if more:
            near(1, 0, 1)
        rank_blocks(4, 6)
    far(0, 2, PIECES)
    if more:
        near(1, 1, 2)
    for d, h, k in routed:
        if d not in chips:
            gather_a.take(d, h, k)
    if len(chips) == 2:
        rank_blocks(6, 7)
        gather_a.take_core(6)
        rank_blocks(7, 8)
    else:
        for d in range(2, V, 2):
            gather_a.take_core(d)
        rank_blocks(2, V)

    def rup_copy(i):
        return pltpu.make_async_remote_copy(
            src_ref=rank_send_up.at[cut(i)], dst_ref=rank_up.at[cut(i)],
            send_sem=rup_send.at[i], recv_sem=rup_recv.at[i],
            device_id=(v, lax.rem(p + 1, K)), device_id_type=MESH,
        )

    def rdn_copy(i):
        return pltpu.make_async_remote_copy(
            src_ref=rank_send_dn.at[cut(i)], dst_ref=rank_dn.at[cut(i)],
            send_sem=rdn_send.at[i], recv_sem=rdn_recv.at[i],
            device_id=(v, lax.rem(p + K - 1, K)), device_id_type=MESH,
        )

    @pl.when(first)
    def _():
        rank_send_up[...] = rank[...].astype(jnp.bfloat16)
        for i in range(PIECES):
            rup_copy(i).start()

    @pl.when(last)
    def _():
        rank_send_dn[...] = rank[...].astype(jnp.bfloat16)
        for i in range(PIECES):
            rdn_copy(i).start()

    @pl.when(first)
    def _():
        for i in range(PIECES):
            up_copy(1, i).start()

    @pl.when(last)
    def _():
        for i in range(PIECES):
            dn_copy(K - 2, i).start()

    gather_b.begin()
    gather_b.second()
    if more:
        near(1, 2, 3)

    def rank_up_step(i):
        @pl.when(p > 0)
        def _():
            rup_copy(i).wait_recv()

            @pl.when(p < K - 1)
            def _():
                rank_send_up[cut(i)] = (
                    rank[cut(i)] + rank_up[cut(i)].astype(jnp.float32)
                ).astype(jnp.bfloat16)
                rup_copy(i).start()

    def rank_dn_step(i):
        @pl.when(p < K - 1)
        def _():
            rdn_copy(i).wait_recv()

            @pl.when(p > 0)
            def _():
                rank_send_dn[cut(i)] = (
                    rank[cut(i)] + rank_dn[cut(i)].astype(jnp.float32)
                ).astype(jnp.bfloat16)
                rdn_copy(i).start()

    def rank_turn(turn):
        @pl.loop(0, PIECES)
        def _(i):
            @pl.when(low_half if turn == 0 else jnp.logical_not(low_half))
            def _():
                rank_up_step(i)

            @pl.when(jnp.logical_not(low_half) if turn == 0 else low_half)
            def _():
                rank_dn_step(i)

    rank_turn(0)
    for d, h, k in direct:
        gather_b.take(d, h, k)
    rank_turn(1)
    if more:
        near(1, 3, PIECES)
        far(1, 0, PIECES)
    for step in range(2, K - 2):
        near(step, 0, PIECES)
        far(step, 0, PIECES)
    for d, h, k in routed:
        gather_b.take(d, h, k)
    for d in range(0, V, 2):
        gather_b.take_core(d)

    @pl.loop(0, PIECES)
    def _(i):
        @pl.when(p > 0)
        def _():
            rank[cut(i)] += rank_up[cut(i)].astype(jnp.float32)

        @pl.when(p < K - 1)
        def _():
            rank[cut(i)] += rank_dn[cut(i)].astype(jnp.float32)

        low = rank[cut(i)].astype(jnp.bfloat16)
        zero = jnp.zeros_like(low)
        wide = jnp.concatenate(
            [
                jnp.where(owner_mask(o, j, i, piece, R), low, zero)
                for o in range(V)
                for j in range(var_dev)
            ],
            axis=1,
        )
        delta = jnp.dot(
            wide, b_all[...].reshape(V * var_dev * R, cols), preferred_element_type=jnp.float32
        ).astype(jnp.bfloat16)
        total[cut(i)] = delta.astype(jnp.float32) + part[p, cut(i)].astype(jnp.float32)

    def last_up(i):
        @pl.when(p > 0)
        def _():
            up_copy(p, i).wait_recv()
            total[cut(i)] += recv_up[p, cut(i)].astype(jnp.float32)

    def last_dn(i):
        @pl.when(p < K - 1)
        def _():
            dn_copy(p, i).wait_recv()
            total[cut(i)] += recv_dn[p, cut(i)].astype(jnp.float32)

    @pl.loop(0, PIECES)
    def _(i):
        @pl.when(low_half)
        def _():
            last_dn(i)

        @pl.when(jnp.logical_not(low_half))
        def _():
            last_up(i)

    @pl.loop(0, PIECES)
    def _(i):
        @pl.when(low_half)
        def _():
            last_up(i)

        @pl.when(jnp.logical_not(low_half))
        def _():
            last_dn(i)

        out[cut(i)] = total[cut(i)].astype(jnp.bfloat16)

    for copy in pending:
        copy.wait_send()

    @pl.loop(0, PIECES)
    def _(i):
        for c in range(K):
            @pl.when(p < c)
            def _():
                up_copy(c, i).wait_send()

            @pl.when(p > c)
            def _():
                dn_copy(c, i).wait_send()

        @pl.when(p < K - 1)
        def _():
            rup_copy(i).wait_send()

        @pl.when(p > 0)
        def _():
            rdn_copy(i).wait_send()


def body(V, K, tokens, kv_weight, factor_a, factor_scale, factor_b, counts):
    rows, feats = tokens.shape
    wide = kv_weight.shape[1]
    cols = wide // K
    var_dev, _, R = factor_a.shape
    DMA = pltpu.SemaphoreType.DMA
    bf16, f32 = jnp.bfloat16, jnp.float32
    anywhere = pl.BlockSpec(memory_space=pl.ANY)
    sends = 2 * (V // 2 - 1)
    halves = (2, V // 2)
    gather_sems = [DMA((sends,)), DMA(halves), DMA(halves), DMA(halves)]
    chain = [DMA((K, PIECES)), DMA((K, PIECES))]
    rank_chain = [DMA((PIECES,)), DMA((PIECES,))]
    return pl.pallas_call(
        functools.partial(kernel, V, K),
        out_shape=pltpu.VMEM((rows, cols), bf16),
        in_specs=[
            anywhere, anywhere, anywhere, anywhere, anywhere, anywhere,
        ],
        out_specs=pl.BlockSpec(memory_space=pltpu.VMEM),
        scratch_shapes=[
            pltpu.VMEM((rows, feats), bf16),
            pltpu.VMEM((K, feats, cols), bf16),
            pltpu.VMEM((V, var_dev, feats, R), bf16),
            pltpu.VMEM((var_dev, R, cols), bf16),
            pltpu.VMEM((V, var_dev, R, cols), bf16),
            pltpu.VMEM((K, rows, cols), bf16),
            pltpu.VMEM((K, rows, cols), bf16),
            pltpu.VMEM((K, rows, cols), bf16),
            pltpu.VMEM((rows, R), f32),
            pltpu.VMEM((rows, R), bf16),
            pltpu.VMEM((rows, R), bf16),
            pltpu.VMEM((rows, R), bf16),
            pltpu.VMEM((rows, R), bf16),
            pltpu.VMEM((rows, cols), f32),
            pltpu.VMEM(factor_scale.shape, bf16),
            pltpu.SMEM(counts.shape, jnp.int32),
            pltpu.SMEM((V * var_dev + 1,), jnp.int32),
            DMA((PIECES + 1,)), DMA((K + 1,)), DMA((4,)),
            *gather_sems, *gather_sems, *chain, *chain, *rank_chain, *rank_chain,
        ],
        compiler_params=pltpu.CompilerParams(
            collective_id=0, has_side_effects=True, vmem_limit_bytes=60 << 20
        ),
    )(tokens, kv_weight, factor_a, factor_scale, factor_b, counts)


def solution(mesh):
    return jax.shard_map(
        functools.partial(body, mesh.shape["var"], mesh.shape["tp"]),
        mesh=mesh,
        in_specs=(
            P("var", "tp"),
            P("tp", None),
            P("var", "tp", None),
            P("var", None),
            P("var", None, "tp"),
            P(),
        ),
        out_specs=P("var", "tp"),
        check_vma=False,
    )
```

```python
import functools

import jax
import jax.numpy as jnp
from jax import lax
from jax.experimental import pallas as pl
from jax.experimental.pallas import tpu as pltpu
from jax.sharding import PartitionSpec as P

MESH = pl.DeviceIdType.MESH
PIECES = 4


def span(masks):
    found = [0]
    for mask in masks:
        found = found + [old ^ mask for old in found]
    return found


def kernel(
    V, K,
    tok_hbm, w_hbm, a_hbm, scale_hbm, b_hbm, counts_hbm,
    out,
    tok, w, a_all, b_raw, b_all, part, recv_up, recv_dn, rank, rank_up, rank_dn, rank_send_up,
    rank_send_dn, total, scale_ref, counts_ref, ends,
    tok_sem, w_sem, own_sem,
    sent, a_recv, a_core_recv, b_recv, b_core_recv,
    up_recv, dn_recv, last_recv, rup_recv, rdn_recv,
):
    v = lax.axis_index("var")
    p = lax.axis_index("tp")
    rows, feats = tok.shape
    cols = w.shape[2]
    var_dev = a_all.shape[1]
    R = a_all.shape[3]
    piece = rows // PIECES
    first, last = p == 0, p == K - 1
    low_half = p < K // 2

    def cut(i):
        return pl.ds(pl.multiple_of(i * piece, piece), piece)

    def chunk_at(k):
        c = k // 2
        c = jnp.where(k % 2 == 0, K - 1 - c, c)
        return jnp.where(low_half, c, K - 1 - c)

    other = pl.ds(piece, rows - piece)
    tok_rest = pltpu.make_async_copy(tok_hbm.at[other], tok.at[other], tok_sem.at[2])

    def w_copy(k):
        c = chunk_at(k)
        return pltpu.make_async_copy(
            w_hbm.at[:, pl.ds(pl.multiple_of(c * cols, cols), cols)], w.at[c], w_sem.at[k]
        )

    half_cols = cols // 2

    def w_half(h):
        at = pl.multiple_of(chunk_at(0) * cols + h * half_cols, half_cols)
        return pltpu.make_async_copy(
            w_hbm.at[:, pl.ds(at, half_cols)],
            w.at[chunk_at(0), :, pl.ds(h * half_cols, half_cols)],
            w_sem.at[0 if h == 0 else K],
        )

    sub = piece // 2

    def tok_sub(i):
        here = pl.ds(i * sub, sub)
        return pltpu.make_async_copy(tok_hbm.at[here], tok.at[here], tok_sem.at[i])

    w_half(0).start()
    tok_sub(0).start()
    tok_sub(1).start()
    w_half(1).start()
    own_a = pltpu.make_async_copy(a_hbm, a_all.at[v], own_sem.at[0])
    own_b = pltpu.make_async_copy(b_hbm, b_raw, own_sem.at[1])
    own_scale = pltpu.make_async_copy(scale_hbm, scale_ref, own_sem.at[2])
    own_counts = pltpu.make_async_copy(counts_hbm, counts_ref, own_sem.at[3])

    masks = []
    m = 1
    while m < V:
        masks.append(m)
        m *= 2
    barrier = pltpu.get_barrier_semaphore()
    for m in masks:
        pl.semaphore_signal(barrier, inc=1, device_id=(lax.bitwise_xor(v, m), p), device_id_type=MESH)

    @pl.when(p > 0)
    def _():
        pl.semaphore_signal(barrier, inc=1, device_id=(v, p - 1), device_id_type=MESH)

    @pl.when(p < K - 1)
    def _():
        pl.semaphore_signal(barrier, inc=1, device_id=(v, p + 1), device_id_type=MESH)

    def base(c, i):
        part[c, cut(i)] = jnp.dot(
            tok[cut(i)], w[c], preferred_element_type=jnp.float32
        ).astype(jnp.bfloat16)

    tok_sub(0).wait()
    w_half(0).wait()
    tok_rest.start()
    for k in range(1, K):
        w_copy(k).start()
    own_counts.start()
    own_scale.start()
    own_a.start()
    own_b.start()

    pl.semaphore_wait(
        barrier, len(masks) + (p > 0).astype(jnp.int32) + (p < K - 1).astype(jnp.int32)
    )

    chips = masks[1:]
    orders = (chips, chips[::-1])

    def half(ref, h):
        size = ref.shape[1] // 2
        return ref.at[:, pl.ds(h * size, size)]

    class Gather:
        def __init__(self, own, everything, send, recv, core_recv):
            self.own, self.all = own, everything
            self.send, self.recv, self.core_recv = send, recv, core_recv

        def copy(self, src, dst, recv, to):
            return pltpu.make_async_remote_copy(
                src_ref=src, dst_ref=dst, send_sem=self.send, recv_sem=recv,
                device_id=(lax.bitwise_xor(v, to), p), device_id_type=MESH,
            )

        def block(self, d, h):
            if d == 0 and self.own is not None:
                return half(self.own, h)
            return half(self.all.at[lax.bitwise_xor(v, d)], h)

        def target(self, d, h):
            return half(self.all.at[lax.bitwise_xor(v, d)], h)

        def to_chip(self, d, h, k):
            m = orders[h][k]
            recv = self.recv.at[h, (d ^ m) // 2 - 1]
            self.copy(self.block(d, h), self.target(d, h), recv, m).start()

        def to_core(self, d, h):
            self.copy(self.block(d, h), self.target(d, h), self.core_recv.at[d // 2], 1).start()

        def begin(self):
            for h in range(2):
                self.to_chip(0, h, 0)
            for h in range(2):
                self.to_core(0, h)

        def second(self):
            for k in range(1, len(chips)):
                for h in range(2):
                    self.to_chip(0, h, k)

        def take(self, d, h, k):
            got = self.target(d, h)
            self.copy(got, got, self.recv.at[h, d // 2 - 1], 1).wait_recv()
            for later in range(k + 1, len(chips)):
                self.to_chip(d, h, later)
            self.to_core(d, h)

        def take_core(self, d):
            got = self.all.at[lax.bitwise_xor(v, d ^ 1)]
            self.copy(got, got, self.core_recv.at[d // 2], 1).wait_recv()

        def wait_sent(self):
            every = self.all.at[pl.ds(0, V - 1)]
            self.copy(every, every, self.core_recv.at[0], 1).wait_send()

    gather_a = Gather(a_hbm, a_all, sent.at[0], a_recv, a_core_recv)
    gather_b = Gather(None, b_all, sent.at[1], b_recv, b_core_recv)

    def leg(i):
        return pl.ds(pl.multiple_of(i * (2 * piece), 2 * piece), 2 * piece)

    def chain_copy(dst, c, here, there, recv, step):
        return pltpu.make_async_remote_copy(
            src_ref=part.at[c, here, there], dst_ref=dst.at[c, here, there],
            send_sem=sent.at[2], recv_sem=recv,
            device_id=(v, lax.rem(p + step, K)), device_id_type=MESH,
        )

    full = pl.ds(0, cols)

    def up_copy(c, i, here=None, there=full):
        return chain_copy(recv_up, c, leg(i) if here is None else here, there, up_recv.at[c - 2, i], 1)

    def dn_copy(c, i, here=None, there=full):
        return chain_copy(recv_dn, c, leg(i) if here is None else here, there, dn_recv.at[c, i], K - 1)

    def up_last(i):
        return chain_copy(recv_up, 1, cut(i), full, last_recv.at[i], 1)

    def dn_last(i):
        return chain_copy(recv_dn, K - 2, cut(i), full, last_recv.at[i], K - 1)

    def send_early(c, i, here=None):
        @pl.when(first & (c >= 2))
        def _():
            up_copy(c, i, here).start()

        @pl.when(last & (c <= K - 3))
        def _():
            dn_copy(c, i, here).start()

    def opening(here, h):
        c = chunk_at(0)
        there = pl.ds(h * half_cols, half_cols)
        part[c, here, there] = jnp.dot(
            tok[here], w[c, :, there], preferred_element_type=jnp.float32
        ).astype(jnp.bfloat16)

        @pl.when(first)
        def _():
            up_copy(c, 0, here, there).start()

        @pl.when(last)
        def _():
            dn_copy(c, 0, here, there).start()

    opening(pl.ds(0, sub), 0)
    tok_sub(1).wait()
    opening(pl.ds(sub, sub), 0)
    w_half(1).wait()
    opening(pl.ds(0, piece), 1)
    gather_a.begin()
    gather_a.second()

    tok_rest.wait()
    base(chunk_at(0), 1)
    send_early(chunk_at(0), 0, cut(1))

    @pl.loop(2, PIECES)
    def _(i):
        base(chunk_at(0), i)

    send_early(chunk_at(0), 1)

    @pl.loop(1, K)
    def _(k):
        c = chunk_at(k)
        w_copy(k).wait()

        @pl.loop(0, PIECES)
        def _(i):
            base(c, i)

            @pl.when(i % 2 == 1)
            def _():
                send_early(c, i // 2)

    own_counts.wait()
    running = jnp.int32(0)
    ends[0] = running
    for j in range(V * var_dev):
        running = running + counts_ref[v, j]
        ends[j + 1] = running

    own_b.wait()
    own_scale.wait()
    for j in range(var_dev):
        turned = jnp.broadcast_to(scale_ref[j : j + 1, :].astype(jnp.float32), (R, R)).T
        for q in range(cols // R):
            at = pl.ds(q * R, R)
            b_all[v, j, :, at] = (b_raw[j, :, at].astype(jnp.float32) * turned).astype(jnp.bfloat16)

    def owner_mask(o, j, i, size, n):
        at = lax.broadcasted_iota(jnp.int32, (size, n), 0) + i * size
        return (at >= ends[o * var_dev + j]) & (at < ends[o * var_dev + j + 1])

    def rank_blocks(lo, hi, clear=False):
        @pl.loop(lo, hi)
        def _(d):
            o = lax.bitwise_xor(v, d)
            both = jnp.concatenate([a_all[o, j] for j in range(var_dev)], axis=1)
            product = jnp.dot(tok[...], both, preferred_element_type=jnp.float32)
            picked = rank[...]
            if clear:
                picked = jnp.where(d == lo, jnp.zeros_like(picked), picked)
            for j in range(var_dev):
                picked = jnp.where(owner_mask(o, j, 0, rows, R), product[:, j * R : (j + 1) * R], picked)
            rank[...] = picked

    def add_up(c, i):
        @pl.when((p > 0) & (p < c))
        def _():
            up_copy(c, i).wait_recv()
            for half_leg in range(2):
                here = cut(2 * i + half_leg)
                part[c, here] = (
                    part[c, here].astype(jnp.float32) + recv_up[c, here].astype(jnp.float32)
                ).astype(jnp.bfloat16)
            up_copy(c, i).start()

    def add_dn(c, i):
        @pl.when((p < K - 1) & (p > c))
        def _():
            dn_copy(c, i).wait_recv()
            for half_leg in range(2):
                here = cut(2 * i + half_leg)
                part[c, here] = (
                    part[c, here].astype(jnp.float32) + recv_dn[c, here].astype(jnp.float32)
                ).astype(jnp.bfloat16)
            dn_copy(c, i).start()

    def near(step, i):
        @pl.when(low_half)
        def _():
            add_up(K - 1 - step, i)

        @pl.when(jnp.logical_not(low_half))
        def _():
            add_dn(step, i)

    def far(step, i):
        @pl.when(low_half)
        def _():
            add_dn(step, i)

        @pl.when(jnp.logical_not(low_half))
        def _():
            add_up(K - 1 - step, i)

    direct, routed = [], []
    for k in range(len(chips)):
        for h in range(2):
            for t in span(orders[h][:k]):
                (direct if k == 0 else routed).append((orders[h][k] ^ t, h, k))
    more = K > 3
    near(0, 0)
    for d, h, k in direct:
        gather_a.take(d, h, k)
    own_a.wait()
    gather_a.take_core(0)
    rank_blocks(0, 2, clear=True)
    near(0, 1)
    for d, h, k in routed:
        if d in chips:
            gather_a.take(d, h, k)
    if len(chips) == 2:
        gather_a.take_core(2)
        gather_a.take_core(4)
        rank_blocks(2, 4)
        far(0, 0)
        rank_blocks(4, 6)
    else:
        far(0, 0)
    if more:
        near(1, 0)
    for d, h, k in routed:
        if d not in chips:
            gather_a.take(d, h, k)
    if len(chips) == 2:
        rank_blocks(6, 7)
        gather_a.take_core(6)
        rank_blocks(7, 8)
    else:
        for d in range(2, V, 2):
            gather_a.take_core(d)
        rank_blocks(2, V)

    def rup_copy(i):
        return pltpu.make_async_remote_copy(
            src_ref=rank_send_up.at[leg(i)], dst_ref=rank_up.at[leg(i)],
            send_sem=sent.at[3], recv_sem=rup_recv.at[i],
            device_id=(v, lax.rem(p + 1, K)), device_id_type=MESH,
        )

    def rdn_copy(i):
        return pltpu.make_async_remote_copy(
            src_ref=rank_send_dn.at[leg(i)], dst_ref=rank_dn.at[leg(i)],
            send_sem=sent.at[4], recv_sem=rdn_recv.at[i],
            device_id=(v, lax.rem(p + K - 1, K)), device_id_type=MESH,
        )

    @pl.when(first)
    def _():
        rank_send_up[...] = rank[...].astype(jnp.bfloat16)
        for i in range(2):
            rup_copy(i).start()

    @pl.when(last)
    def _():
        rank_send_dn[...] = rank[...].astype(jnp.bfloat16)
        for i in range(2):
            rdn_copy(i).start()

    @pl.when(first)
    def _():
        for i in range(PIECES):
            up_last(i).start()

    @pl.when(last)
    def _():
        for i in range(PIECES):
            dn_last(i).start()

    gather_b.begin()
    gather_b.second()
    far(0, 1)

    def rank_up_step(i):
        @pl.when(p > 0)
        def _():
            rup_copy(i).wait_recv()

            @pl.when(p < K - 1)
            def _():
                rank_send_up[leg(i)] = (
                    rank[leg(i)] + rank_up[leg(i)].astype(jnp.float32)
                ).astype(jnp.bfloat16)
                rup_copy(i).start()

    def rank_dn_step(i):
        @pl.when(p < K - 1)
        def _():
            rdn_copy(i).wait_recv()

            @pl.when(p > 0)
            def _():
                rank_send_dn[leg(i)] = (
                    rank[leg(i)] + rank_dn[leg(i)].astype(jnp.float32)
                ).astype(jnp.bfloat16)
                rdn_copy(i).start()

    def rank_turn(turn):
        @pl.loop(0, 2)
        def _(i):
            @pl.when(low_half if turn == 0 else jnp.logical_not(low_half))
            def _():
                rank_up_step(i)

            @pl.when(jnp.logical_not(low_half) if turn == 0 else low_half)
            def _():
                rank_dn_step(i)

    rank_turn(0)
    for d, h, k in direct:
        gather_b.take(d, h, k)
    rank_turn(1)
    if more:
        near(1, 1)
        far(1, 0)
        far(1, 1)
    for step in range(2, K - 2):
        for i in range(2):
            near(step, i)
            far(step, i)
    for d, h, k in routed:
        gather_b.take(d, h, k)
    for d in range(0, V, 2):
        gather_b.take_core(d)

    @pl.loop(0, PIECES)
    def _(i):
        @pl.when(p > 0)
        def _():
            rank[cut(i)] += rank_up[cut(i)].astype(jnp.float32)

        @pl.when(p < K - 1)
        def _():
            rank[cut(i)] += rank_dn[cut(i)].astype(jnp.float32)

        low = rank[cut(i)].astype(jnp.bfloat16)
        zero = jnp.zeros_like(low)
        wide = jnp.concatenate(
            [
                jnp.where(owner_mask(o, j, i, piece, R), low, zero)
                for o in range(V)
                for j in range(var_dev)
            ],
            axis=1,
        )
        delta = jnp.dot(
            wide, b_all[...].reshape(V * var_dev * R, cols), preferred_element_type=jnp.float32
        ).astype(jnp.bfloat16)
        total[cut(i)] = delta.astype(jnp.float32) + part[p, cut(i)].astype(jnp.float32)

    def more_up(here):
        total[here] += recv_up[p, here].astype(jnp.float32)

    def more_dn(here):
        total[here] += recv_dn[p, here].astype(jnp.float32)

    @pl.loop(0, PIECES)
    def _(i):
        @pl.when(low_half & (p < K - 1))
        def _():
            @pl.when(i % 2 == 0)
            def _():
                dn_copy(p, i // 2).wait_recv()

            more_dn(cut(i))

        @pl.when(jnp.logical_not(low_half) & (p > 0))
        def _():
            @pl.when(i % 2 == 0)
            def _():
                up_copy(p, i // 2).wait_recv()

            more_up(cut(i))

    @pl.loop(0, PIECES)
    def _(i):
        @pl.when(low_half & (p > 0))
        def _():
            @pl.when(p == 1)
            def _():
                up_last(i).wait_recv()

            @pl.when((p > 1) & (i % 2 == 0))
            def _():
                up_copy(p, i // 2).wait_recv()

            more_up(cut(i))

        @pl.when(jnp.logical_not(low_half) & (p < K - 1))
        def _():
            @pl.when(p == K - 2)
            def _():
                dn_last(i).wait_recv()

            @pl.when((p < K - 2) & (i % 2 == 0))
            def _():
                dn_copy(p, i // 2).wait_recv()

            more_dn(cut(i))

        out[cut(i)] = total[cut(i)].astype(jnp.bfloat16)

    gather_a.wait_sent()
    gather_b.wait_sent()

    def wait_sent(src, dst, sem):
        pltpu.make_async_remote_copy(
            src_ref=src, dst_ref=dst, send_sem=sem, recv_sem=last_recv.at[0],
            device_id=(lax.bitwise_xor(v, 1), p), device_id_type=MESH,
        ).wait_send()

    each = pl.ds(0, K - 1)
    wait_sent(part.at[each], recv_up.at[each], sent.at[2])

    @pl.when(p < K - 1)
    def _():
        wait_sent(rank_send_up, rank_up, sent.at[3])

    @pl.when(p > 0)
    def _():
        wait_sent(rank_send_dn, rank_dn, sent.at[4])


def body(V, K, tokens, kv_weight, factor_a, factor_scale, factor_b, counts):
    rows, feats = tokens.shape
    wide = kv_weight.shape[1]
    cols = wide // K
    var_dev, _, R = factor_a.shape
    DMA = pltpu.SemaphoreType.DMA
    bf16, f32 = jnp.bfloat16, jnp.float32
    anywhere = pl.BlockSpec(memory_space=pl.ANY)
    gather_sems = [DMA((2, V // 2 - 1)), DMA((V // 2,))]
    return pl.pallas_call(
        functools.partial(kernel, V, K),
        out_shape=pltpu.VMEM((rows, cols), bf16),
        in_specs=[
            anywhere, anywhere, anywhere, anywhere, anywhere, anywhere,
        ],
        out_specs=pl.BlockSpec(memory_space=pltpu.VMEM),
        scratch_shapes=[
            pltpu.VMEM((rows, feats), bf16),
            pltpu.VMEM((K, feats, cols), bf16),
            pltpu.VMEM((V, var_dev, feats, R), bf16),
            pltpu.VMEM((var_dev, R, cols), bf16),
            pltpu.VMEM((V, var_dev, R, cols), bf16),
            pltpu.VMEM((K, rows, cols), bf16),
            pltpu.VMEM((K, rows, cols), bf16),
            pltpu.VMEM((K, rows, cols), bf16),
            pltpu.VMEM((rows, R), f32),
            pltpu.VMEM((rows, R), bf16),
            pltpu.VMEM((rows, R), bf16),
            pltpu.VMEM((rows, R), bf16),
            pltpu.VMEM((rows, R), bf16),
            pltpu.VMEM((rows, cols), f32),
            pltpu.VMEM(factor_scale.shape, bf16),
            pltpu.SMEM(counts.shape, jnp.int32),
            pltpu.SMEM((V * var_dev + 1,), jnp.int32),
            DMA((3,)), DMA((K + 1,)), DMA((4,)), DMA((5,)), *gather_sems, *gather_sems,
            DMA((K - 2, 2)), DMA((K - 2, 2)), DMA((PIECES,)), DMA((2,)), DMA((2,)),
        ],
        compiler_params=pltpu.CompilerParams(
            collective_id=0, has_side_effects=True, vmem_limit_bytes=60 << 20
        ),
    )(tokens, kv_weight, factor_a, factor_scale, factor_b, counts)


def solution(mesh):
    return jax.shard_map(
        functools.partial(body, mesh.shape["var"], mesh.shape["tp"]),
        mesh=mesh,
        in_specs=(
            P("var", "tp"),
            P("tp", None),
            P("var", "tp", None),
            P("var", None),
            P("var", None, "tp"),
            P(),
        ),
        out_specs=P("var", "tp"),
        check_vma=False,
    )
```

```python
import functools

import jax
import jax.numpy as jnp
from jax import lax
from jax.experimental import pallas as pl
from jax.experimental.pallas import tpu as pltpu
from jax.sharding import PartitionSpec as P

MESH = pl.DeviceIdType.MESH
PIECES = 4


def span(masks):
    found = [0]
    for mask in masks:
        found = found + [old ^ mask for old in found]
    return found


def kernel(
    V, K,
    tok_hbm, w_hbm, a_hbm, scale_hbm, b_hbm, counts_hbm,
    out,
    tok, w, a_all, b_raw, b_all, part, recv_up, recv_dn, rank, rank_up, rank_dn, rank_send_up,
    rank_send_dn, total, scale_ref, counts_ref, ends,
    tok_sem, w_sem, own_sem,
    a_recv, a_core_recv, b_recv, b_core_recv,
    up_recv, dn_recv, last_recv, rup_recv, rdn_recv,
):
    sent = (tok_sem.at[0], own_sem.at[0], w_sem.at[0], tok_sem.at[1], tok_sem.at[2])
    v = lax.axis_index("var")
    p = lax.axis_index("tp")
    rows, feats = tok.shape
    cols = w.shape[2]
    var_dev = a_all.shape[1]
    R = a_all.shape[3]
    piece = rows // PIECES
    first, last = p == 0, p == K - 1
    low_half = p < K // 2

    def cut(i):
        return pl.ds(pl.multiple_of(i * piece, piece), piece)

    def chunk_at(k):
        c = k // 2
        c = jnp.where(k % 2 == 0, K - 1 - c, c)
        return jnp.where(low_half, c, K - 1 - c)

    other = pl.ds(piece, rows - piece)
    tok_rest = pltpu.make_async_copy(tok_hbm.at[other], tok.at[other], tok_sem.at[2])

    def w_copy(k):
        c = chunk_at(k)
        return pltpu.make_async_copy(
            w_hbm.at[:, pl.ds(pl.multiple_of(c * cols, cols), cols)], w.at[c], w_sem.at[2]
        )

    half_cols = cols // 2

    def w_half(h):
        at = pl.multiple_of(chunk_at(0) * cols + h * half_cols, half_cols)
        return pltpu.make_async_copy(
            w_hbm.at[:, pl.ds(at, half_cols)],
            w.at[chunk_at(0), :, pl.ds(h * half_cols, half_cols)],
            w_sem.at[h],
        )

    sub = piece // 2

    def tok_sub(i):
        here = pl.ds(i * sub, sub)
        return pltpu.make_async_copy(tok_hbm.at[here], tok.at[here], tok_sem.at[i])

    masks = []
    m = 1
    while m < V:
        masks.append(m)
        m *= 2
    barrier = pltpu.get_barrier_semaphore()
    for m in masks:
        pl.semaphore_signal(barrier, inc=1, device_id=(lax.bitwise_xor(v, m), p), device_id_type=MESH)

    @pl.when(p > 0)
    def _():
        pl.semaphore_signal(barrier, inc=1, device_id=(v, p - 1), device_id_type=MESH)

    @pl.when(p < K - 1)
    def _():
        pl.semaphore_signal(barrier, inc=1, device_id=(v, p + 1), device_id_type=MESH)

    w_half(0).start()
    tok_sub(0).start()
    tok_sub(1).start()
    w_half(1).start()
    own_a = pltpu.make_async_copy(a_hbm, a_all.at[v], own_sem.at[0])
    own_b = pltpu.make_async_copy(b_hbm, b_raw, own_sem.at[1])
    own_scale = pltpu.make_async_copy(scale_hbm, scale_ref, own_sem.at[2])
    own_counts = pltpu.make_async_copy(counts_hbm, counts_ref, own_sem.at[3])

    def base(c, i):
        part[c, cut(i)] = jnp.dot(
            tok[cut(i)], w[c], preferred_element_type=jnp.float32
        ).astype(jnp.bfloat16)

    tok_sub(0).wait()
    w_half(0).wait()
    tok_rest.start()
    for k in range(1, K):
        w_copy(k).start()
    own_counts.start()
    own_scale.start()
    own_a.start()
    own_b.start()

    pl.semaphore_wait(
        barrier, len(masks) + (p > 0).astype(jnp.int32) + (p < K - 1).astype(jnp.int32)
    )

    chips = masks[1:]
    orders = (chips, chips[::-1])

    def half(ref, h):
        size = ref.shape[1] // 2
        return ref.at[:, pl.ds(h * size, size)]

    class Gather:
        def __init__(self, own, everything, send, recv, core_recv, apart):
            self.own, self.all, self.apart = own, everything, apart
            self.send, self.recv, self.core_recv = send, recv, core_recv

        def copy(self, src, dst, recv, to):
            return pltpu.make_async_remote_copy(
                src_ref=src, dst_ref=dst, send_sem=self.send, recv_sem=recv,
                device_id=(lax.bitwise_xor(v, to), p), device_id_type=MESH,
            )

        def block(self, d, h):
            if d == 0 and self.own is not None:
                return half(self.own, h)
            return half(self.all.at[lax.bitwise_xor(v, d)], h)

        def target(self, d, h):
            return half(self.all.at[lax.bitwise_xor(v, d)], h)

        def to_chip(self, d, h, k):
            m = orders[h][k]
            recv = self.recv.at[self.group(d ^ m, k)]
            self.copy(self.block(d, h), self.target(d, h), recv, m).start()

        def to_core(self, d, h):
            recv = self.core_recv.at[d // 2 if self.apart else 0]
            self.copy(self.block(d, h), self.target(d, h), recv, 1).start()

        def group(self, d, k):
            return max(2 * k - (d in chips), 0) if self.apart else k

        def begin(self):
            for h in range(2):
                self.to_chip(0, h, 0)
            for h in range(2):
                self.to_core(0, h)

        def second(self):
            for k in range(1, len(chips)):
                for h in range(2):
                    self.to_chip(0, h, k)

        def take(self, group):
            taken = [(d, h, k) for d, h, k in arrivals if self.group(d, k) == group]
            every = self.all.at[pl.ds(0, len(taken) // 2)]
            self.copy(every, every, self.recv.at[group], 1).wait_recv()
            for d, h, k in taken:
                for later in range(k + 1, len(chips)):
                    self.to_chip(d, h, later)
                self.to_core(d, h)

        def take_core(self, d):
            got = self.all.at[lax.bitwise_xor(v, d ^ 1)]
            self.copy(got, got, self.core_recv.at[d // 2], 1).wait_recv()

        def take_cores(self):
            every = self.all.at[pl.ds(0, V // 2)]
            self.copy(every, every, self.core_recv.at[0], 1).wait_recv()

        def wait_sent(self):
            every = self.all.at[pl.ds(0, V - 1)]
            self.copy(every, every, self.core_recv.at[0], 1).wait_send()

    arrivals = [
        (orders[h][k] ^ t, h, k)
        for k in range(len(chips)) for h in range(2) for t in span(orders[h][:k])
    ]
    gather_a = Gather(a_hbm, a_all, sent[0], a_recv, a_core_recv, True)
    gather_b = Gather(None, b_all, sent[1], b_recv, b_core_recv, False)

    def leg(i):
        return pl.ds(pl.multiple_of(i * (2 * piece), 2 * piece), 2 * piece)

    def chain_copy(dst, c, here, there, recv, step):
        return pltpu.make_async_remote_copy(
            src_ref=part.at[c, here, there], dst_ref=dst.at[c, here, there],
            send_sem=sent[2], recv_sem=recv,
            device_id=(v, lax.rem(p + step, K)), device_id_type=MESH,
        )

    full = pl.ds(0, cols)

    def up_copy(c, i, here=None, there=full):
        return chain_copy(recv_up, c, leg(i) if here is None else here, there, up_recv.at[c - 2, i], 1)

    def dn_copy(c, i, here=None, there=full):
        return chain_copy(recv_dn, c, leg(i) if here is None else here, there, dn_recv.at[c, i], K - 1)

    def up_last(i):
        return chain_copy(recv_up, 1, cut(i), full, last_recv.at[i], 1)

    def dn_last(i):
        return chain_copy(recv_dn, K - 2, cut(i), full, last_recv.at[i], K - 1)

    def send_early(c, i, here=None):
        @pl.when(first & (c >= 2))
        def _():
            up_copy(c, i, here).start()

        @pl.when(last & (c <= K - 3))
        def _():
            dn_copy(c, i, here).start()

    def opening(here, h):
        c = chunk_at(0)
        there = pl.ds(h * half_cols, half_cols)
        part[c, here, there] = jnp.dot(
            tok[here], w[c, :, there], preferred_element_type=jnp.float32
        ).astype(jnp.bfloat16)

        @pl.when(first)
        def _():
            up_copy(c, 0, here, there).start()

        @pl.when(last)
        def _():
            dn_copy(c, 0, here, there).start()

    opening(pl.ds(0, sub), 0)
    tok_sub(1).wait()
    opening(pl.ds(sub, sub), 0)
    w_half(1).wait()
    opening(pl.ds(0, piece), 1)
    gather_a.begin()
    gather_a.second()

    tok_rest.wait()
    base(chunk_at(0), 1)
    send_early(chunk_at(0), 0, cut(1))

    @pl.loop(2, PIECES)
    def _(i):
        base(chunk_at(0), i)

    send_early(chunk_at(0), 1)

    others = w.at[pl.ds(0, K - 1)]
    pltpu.make_async_copy(others, others, w_sem.at[2]).wait()

    @pl.loop(1, K)
    def _(k):
        c = chunk_at(k)

        @pl.loop(0, PIECES)
        def _(i):
            base(c, i)

            @pl.when(i % 2 == 1)
            def _():
                send_early(c, i // 2)

    own_counts.wait()
    running = jnp.int32(0)
    ends[0] = running
    for j in range(V * var_dev):
        running = running + counts_ref[v, j]
        ends[j + 1] = running

    own_b.wait()
    own_scale.wait()
    for j in range(var_dev):
        turned = jnp.broadcast_to(scale_ref[j : j + 1, :].astype(jnp.float32), (R, R)).T
        for q in range(cols // R):
            at = pl.ds(q * R, R)
            b_all[v, j, :, at] = (b_raw[j, :, at].astype(jnp.float32) * turned).astype(jnp.bfloat16)

    def owner_mask(o, j, i, size, n):
        at = lax.broadcasted_iota(jnp.int32, (size, n), 0) + i * size
        return (at >= ends[o * var_dev + j]) & (at < ends[o * var_dev + j + 1])

    def rank_blocks(lo, hi, clear=False):
        @pl.loop(lo, hi)
        def _(d):
            o = lax.bitwise_xor(v, d)
            both = jnp.concatenate([a_all[o, j] for j in range(var_dev)], axis=1)
            product = jnp.dot(tok[...], both, preferred_element_type=jnp.float32)
            picked = rank[...]
            if clear:
                picked = jnp.where(d == lo, jnp.zeros_like(picked), picked)
            for j in range(var_dev):
                picked = jnp.where(owner_mask(o, j, 0, rows, R), product[:, j * R : (j + 1) * R], picked)
            rank[...] = picked

    def add_up(c, i):
        @pl.when((p > 0) & (p < c))
        def _():
            up_copy(c, i).wait_recv()
            for half_leg in range(2):
                here = cut(2 * i + half_leg)
                part[c, here] = (
                    part[c, here].astype(jnp.float32) + recv_up[c, here].astype(jnp.float32)
                ).astype(jnp.bfloat16)
            up_copy(c, i).start()

    def add_dn(c, i):
        @pl.when((p < K - 1) & (p > c))
        def _():
            dn_copy(c, i).wait_recv()
            for half_leg in range(2):
                here = cut(2 * i + half_leg)
                part[c, here] = (
                    part[c, here].astype(jnp.float32) + recv_dn[c, here].astype(jnp.float32)
                ).astype(jnp.bfloat16)
            dn_copy(c, i).start()

    def near(step, i):
        @pl.when(low_half)
        def _():
            add_up(K - 1 - step, i)

        @pl.when(jnp.logical_not(low_half))
        def _():
            add_dn(step, i)

    def far(step, i):
        @pl.when(low_half)
        def _():
            add_dn(step, i)

        @pl.when(jnp.logical_not(low_half))
        def _():
            add_up(K - 1 - step, i)

    more = K > 3
    near(0, 0)
    gather_a.take(0)
    own_a.wait()
    gather_a.take_core(0)
    rank_blocks(0, 2, clear=True)
    near(0, 1)
    for k in range(1, len(chips) - 1):
        gather_a.take(2 * k - 1)
        gather_a.take(2 * k)
    gather_a.take(2 * len(chips) - 3)
    if len(chips) == 2:
        gather_a.take_core(2)
        gather_a.take_core(4)
        rank_blocks(2, 4)
        far(0, 0)
        rank_blocks(4, 6)
    else:
        far(0, 0)
    if more:
        near(1, 0)
    gather_a.take(2 * len(chips) - 2)
    if len(chips) == 2:
        rank_blocks(6, 7)
        gather_a.take_core(6)
        rank_blocks(7, 8)
    else:
        for d in range(2, V, 2):
            gather_a.take_core(d)
        rank_blocks(2, V)

    def rup_copy(i):
        return pltpu.make_async_remote_copy(
            src_ref=rank_send_up.at[leg(i)], dst_ref=rank_up.at[leg(i)],
            send_sem=sent[3], recv_sem=rup_recv.at[i],
            device_id=(v, lax.rem(p + 1, K)), device_id_type=MESH,
        )

    def rdn_copy(i):
        return pltpu.make_async_remote_copy(
            src_ref=rank_send_dn.at[leg(i)], dst_ref=rank_dn.at[leg(i)],
            send_sem=sent[4], recv_sem=rdn_recv.at[i],
            device_id=(v, lax.rem(p + K - 1, K)), device_id_type=MESH,
        )

    @pl.when(first)
    def _():
        rank_send_up[...] = rank[...].astype(jnp.bfloat16)
        for i in range(2):
            rup_copy(i).start()

    @pl.when(last)
    def _():
        rank_send_dn[...] = rank[...].astype(jnp.bfloat16)
        for i in range(2):
            rdn_copy(i).start()

    @pl.when(first)
    def _():
        for i in range(PIECES):
            up_last(i).start()

    @pl.when(last)
    def _():
        for i in range(PIECES):
            dn_last(i).start()

    gather_b.begin()
    gather_b.second()
    far(0, 1)

    def rank_up_step(i):
        @pl.when(p > 0)
        def _():
            rup_copy(i).wait_recv()

            @pl.when(p < K - 1)
            def _():
                rank_send_up[leg(i)] = (
                    rank[leg(i)] + rank_up[leg(i)].astype(jnp.float32)
                ).astype(jnp.bfloat16)
                rup_copy(i).start()

    def rank_dn_step(i):
        @pl.when(p < K - 1)
        def _():
            rdn_copy(i).wait_recv()

            @pl.when(p > 0)
            def _():
                rank_send_dn[leg(i)] = (
                    rank[leg(i)] + rank_dn[leg(i)].astype(jnp.float32)
                ).astype(jnp.bfloat16)
                rdn_copy(i).start()

    def rank_turn(turn):
        @pl.loop(0, 2)
        def _(i):
            @pl.when(low_half if turn == 0 else jnp.logical_not(low_half))
            def _():
                rank_up_step(i)

            @pl.when(jnp.logical_not(low_half) if turn == 0 else low_half)
            def _():
                rank_dn_step(i)

    rank_turn(0)
    gather_b.take(0)
    rank_turn(1)
    if more:
        near(1, 1)
        far(1, 0)
        far(1, 1)
    for step in range(2, K - 2):
        for i in range(2):
            near(step, i)
            far(step, i)
    for k in range(1, len(chips)):
        gather_b.take(k)
    gather_b.take_cores()

    @pl.loop(0, PIECES)
    def _(i):
        @pl.when(p > 0)
        def _():
            rank[cut(i)] += rank_up[cut(i)].astype(jnp.float32)

        @pl.when(p < K - 1)
        def _():
            rank[cut(i)] += rank_dn[cut(i)].astype(jnp.float32)

        low = rank[cut(i)].astype(jnp.bfloat16)
        zero = jnp.zeros_like(low)
        wide = jnp.concatenate(
            [
                jnp.where(owner_mask(o, j, i, piece, R), low, zero)
                for o in range(V)
                for j in range(var_dev)
            ],
            axis=1,
        )
        delta = jnp.dot(
            wide, b_all[...].reshape(V * var_dev * R, cols), preferred_element_type=jnp.float32
        ).astype(jnp.bfloat16)
        total[cut(i)] = delta.astype(jnp.float32) + part[p, cut(i)].astype(jnp.float32)

    def more_up(here):
        total[here] += recv_up[p, here].astype(jnp.float32)

    def more_dn(here):
        total[here] += recv_dn[p, here].astype(jnp.float32)

    @pl.loop(0, PIECES)
    def _(i):
        @pl.when(low_half & (p < K - 1))
        def _():
            @pl.when(i % 2 == 0)
            def _():
                dn_copy(p, i // 2).wait_recv()

            more_dn(cut(i))

        @pl.when(jnp.logical_not(low_half) & (p > 0))
        def _():
            @pl.when(i % 2 == 0)
            def _():
                up_copy(p, i // 2).wait_recv()

            more_up(cut(i))

    @pl.loop(0, PIECES)
    def _(i):
        @pl.when(low_half & (p > 0))
        def _():
            @pl.when(p == 1)
            def _():
                up_last(i).wait_recv()

            @pl.when((p > 1) & (i % 2 == 0))
            def _():
                up_copy(p, i // 2).wait_recv()

            more_up(cut(i))

        @pl.when(jnp.logical_not(low_half) & (p < K - 1))
        def _():
            @pl.when(p == K - 2)
            def _():
                dn_last(i).wait_recv()

            @pl.when((p < K - 2) & (i % 2 == 0))
            def _():
                dn_copy(p, i // 2).wait_recv()

            more_dn(cut(i))

        out[cut(i)] = total[cut(i)].astype(jnp.bfloat16)

    gather_a.wait_sent()
    gather_b.wait_sent()

    def wait_sent(src, dst, sem):
        pltpu.make_async_remote_copy(
            src_ref=src, dst_ref=dst, send_sem=sem, recv_sem=last_recv.at[0],
            device_id=(lax.bitwise_xor(v, 1), p), device_id_type=MESH,
        ).wait_send()

    each = pl.ds(0, K - 1)
    wait_sent(part.at[each], recv_up.at[each], sent[2])

    @pl.when(p < K - 1)
    def _():
        wait_sent(rank_send_up, rank_up, sent[3])

    @pl.when(p > 0)
    def _():
        wait_sent(rank_send_dn, rank_dn, sent[4])


def body(V, K, tokens, kv_weight, factor_a, factor_scale, factor_b, counts):
    rows, feats = tokens.shape
    wide = kv_weight.shape[1]
    cols = wide // K
    var_dev, _, R = factor_a.shape
    DMA = pltpu.SemaphoreType.DMA
    bf16, f32 = jnp.bfloat16, jnp.float32
    anywhere = pl.BlockSpec(memory_space=pl.ANY)
    steps = (V // 2).bit_length() - 1
    return pl.pallas_call(
        functools.partial(kernel, V, K),
        out_shape=pltpu.VMEM((rows, cols), bf16),
        in_specs=[
            anywhere, anywhere, anywhere, anywhere, anywhere, anywhere,
        ],
        out_specs=pl.BlockSpec(memory_space=pltpu.VMEM),
        scratch_shapes=[
            pltpu.VMEM((rows, feats), bf16),
            pltpu.VMEM((K, feats, cols), bf16),
            pltpu.VMEM((V, var_dev, feats, R), bf16),
            pltpu.VMEM((var_dev, R, cols), bf16),
            pltpu.VMEM((V, var_dev, R, cols), bf16),
            pltpu.VMEM((K, rows, cols), bf16),
            pltpu.VMEM((K, rows, cols), bf16),
            pltpu.VMEM((K, rows, cols), bf16),
            pltpu.VMEM((rows, R), f32),
            pltpu.VMEM((rows, R), bf16),
            pltpu.VMEM((rows, R), bf16),
            pltpu.VMEM((rows, R), bf16),
            pltpu.VMEM((rows, R), bf16),
            pltpu.VMEM((rows, cols), f32),
            pltpu.VMEM(factor_scale.shape, bf16),
            pltpu.SMEM(counts.shape, jnp.int32),
            pltpu.SMEM((V * var_dev + 1,), jnp.int32),
            DMA((3,)), DMA((3,)), DMA((4,)),
            DMA((2 * steps - 1,)), DMA((V // 2,)), DMA((steps,)), DMA((1,)),
            DMA((K - 2, 2)), DMA((K - 2, 2)), DMA((PIECES,)), DMA((2,)), DMA((2,)),
        ],
        compiler_params=pltpu.CompilerParams(
            collective_id=0, has_side_effects=True, vmem_limit_bytes=60 << 20
        ),
    )(tokens, kv_weight, factor_a, factor_scale, factor_b, counts)


def solution(mesh):
    return jax.shard_map(
        functools.partial(body, mesh.shape["var"], mesh.shape["tp"]),
        mesh=mesh,
        in_specs=(
            P("var", "tp"),
            P("tp", None),
            P("var", "tp", None),
            P("var", None),
            P("var", None, "tp"),
            P(),
        ),
        out_specs=P("var", "tp"),
        check_vma=False,
    )
```

```python
import functools

import jax
import jax.numpy as jnp
from jax import lax
from jax.experimental import pallas as pl
from jax.experimental.pallas import tpu as pltpu
from jax.sharding import PartitionSpec as P

MESH = pl.DeviceIdType.MESH
PIECES = 4


def span(masks):
    found = [0]
    for mask in masks:
        found = found + [old ^ mask for old in found]
    return found


def kernel(
    V, K,
    tok_hbm, w_hbm, a_hbm, scale_hbm, b_hbm, counts_hbm,
    out,
    tok, w, a_all, b_raw, b_all, part, recv_up, recv_dn, rank, rank_up, rank_dn, rank_send_up,
    rank_send_dn, total, scale_ref, counts_ref, ends,
    tok_sem, w_sem, own_sem,
    a_recv, a_core_recv, b_recv, b_core_recv,
    up_recv, dn_recv, last_recv, rup_recv, rdn_recv,
):
    sent = (tok_sem.at[0], own_sem.at[0], w_sem.at[0], tok_sem.at[1], tok_sem.at[2])
    v = lax.axis_index("var")
    p = lax.axis_index("tp")
    rows, feats = tok.shape
    cols = w.shape[2]
    var_dev = a_all.shape[1]
    R = a_all.shape[3]
    piece = rows // PIECES
    first, last = p == 0, p == K - 1
    low_half = p < K // 2
    edge = first | last

    def cut(i):
        return pl.ds(pl.multiple_of(i * piece, piece), piece)

    def chunk_at(k):
        c = k // 2
        c = jnp.where(k % 2 == 0, K - 1 - c, c)
        return jnp.where(low_half, c, K - 1 - c)

    other = pl.ds(piece, rows - piece)
    tok_rest = pltpu.make_async_copy(tok_hbm.at[other], tok.at[other], tok_sem.at[2])

    def w_copy(k):
        c = chunk_at(k)
        return pltpu.make_async_copy(
            w_hbm.at[:, pl.ds(pl.multiple_of(c * cols, cols), cols)], w.at[c], w_sem.at[2]
        )

    half_cols = cols // 2

    def w_half(h):
        at = pl.multiple_of(chunk_at(0) * cols + h * half_cols, half_cols)
        return pltpu.make_async_copy(
            w_hbm.at[:, pl.ds(at, half_cols)],
            w.at[chunk_at(0), :, pl.ds(h * half_cols, half_cols)],
            w_sem.at[h],
        )

    sub = piece // 2

    def tok_sub(i):
        here = pl.ds(i * sub, sub)
        return pltpu.make_async_copy(tok_hbm.at[here], tok.at[here], tok_sem.at[i])

    masks = []
    m = 1
    while m < V:
        masks.append(m)
        m *= 2
    barrier = pltpu.get_barrier_semaphore()
    for m in masks:
        pl.semaphore_signal(barrier, inc=1, device_id=(lax.bitwise_xor(v, m), p), device_id_type=MESH)

    @pl.when(p > 0)
    def _():
        pl.semaphore_signal(barrier, inc=1, device_id=(v, p - 1), device_id_type=MESH)

    @pl.when(p < K - 1)
    def _():
        pl.semaphore_signal(barrier, inc=1, device_id=(v, p + 1), device_id_type=MESH)

    w_half(0).start()
    tok_sub(0).start()
    tok_sub(1).start()
    w_half(1).start()
    own_a = pltpu.make_async_copy(a_hbm, a_all.at[v], own_sem.at[0])
    own_b = pltpu.make_async_copy(b_hbm, b_raw, own_sem.at[1])
    own_scale = pltpu.make_async_copy(scale_hbm, scale_ref, own_sem.at[2])
    own_counts = pltpu.make_async_copy(counts_hbm, counts_ref, own_sem.at[3])

    def base(c, i):
        part[c, cut(i)] = jnp.dot(
            tok[cut(i)], w[c], preferred_element_type=jnp.float32
        ).astype(jnp.bfloat16)

    tok_sub(0).wait()
    w_half(0).wait()
    tok_rest.start()
    for k in range(1, K):
        w_copy(k).start()
    own_counts.start()
    own_scale.start()
    own_a.start()
    own_b.start()

    pl.semaphore_wait(
        barrier, len(masks) + (p > 0).astype(jnp.int32) + (p < K - 1).astype(jnp.int32)
    )

    chips = masks[1:]
    orders = (chips, chips[::-1])

    def half(ref, h):
        size = ref.shape[1] // 2
        return ref.at[:, pl.ds(h * size, size)]

    class Gather:
        def __init__(self, own, everything, send, recv, core_recv, apart):
            self.own, self.all, self.apart = own, everything, apart
            self.send, self.recv, self.core_recv = send, recv, core_recv

        def copy(self, src, dst, recv, to):
            return pltpu.make_async_remote_copy(
                src_ref=src, dst_ref=dst, send_sem=self.send, recv_sem=recv,
                device_id=(lax.bitwise_xor(v, to), p), device_id_type=MESH,
            )

        def block(self, d, h):
            if d == 0 and self.own is not None:
                return half(self.own, h)
            return half(self.all.at[lax.bitwise_xor(v, d)], h)

        def target(self, d, h):
            return half(self.all.at[lax.bitwise_xor(v, d)], h)

        def to_chip(self, d, h, k):
            m = orders[h][k]
            recv = self.recv.at[self.group(d ^ m, k)]
            self.copy(self.block(d, h), self.target(d, h), recv, m).start()

        def to_core(self, d, h):
            recv = self.core_recv.at[d // 2 if self.apart else 0]
            self.copy(self.block(d, h), self.target(d, h), recv, 1).start()

        def group(self, d, k):
            return max(2 * k - (d in chips), 0) if self.apart else k

        def begin(self):
            for h in range(2):
                self.to_chip(0, h, 0)
            for h in range(2):
                self.to_core(0, h)

        def second(self):
            for k in range(1, len(chips)):
                for h in range(2):
                    self.to_chip(0, h, k)

        def take(self, group):
            taken = [(d, h, k) for d, h, k in arrivals if self.group(d, k) == group]
            every = self.all.at[pl.ds(0, len(taken) // 2)]
            self.copy(every, every, self.recv.at[group], 1).wait_recv()
            for d, h, k in taken:
                for later in range(k + 1, len(chips)):
                    self.to_chip(d, h, later)
                self.to_core(d, h)

        def take_core(self, d):
            got = self.all.at[lax.bitwise_xor(v, d ^ 1)]
            self.copy(got, got, self.core_recv.at[d // 2], 1).wait_recv()

        def take_cores(self):
            every = self.all.at[pl.ds(0, V // 2)]
            self.copy(every, every, self.core_recv.at[0], 1).wait_recv()

        def wait_sent(self):
            every = self.all.at[pl.ds(0, V - 1)]
            self.copy(every, every, self.core_recv.at[0], 1).wait_send()

    arrivals = [
        (orders[h][k] ^ t, h, k)
        for k in range(len(chips)) for h in range(2) for t in span(orders[h][:k])
    ]
    gather_a = Gather(a_hbm, a_all, sent[0], a_recv, a_core_recv, True)
    gather_b = Gather(None, b_all, sent[1], b_recv, b_core_recv, False)

    def leg(i):
        return pl.ds(pl.multiple_of(i * (2 * piece), 2 * piece), 2 * piece)

    def chain_copy(dst, c, here, there, recv, step):
        return pltpu.make_async_remote_copy(
            src_ref=part.at[c, here, there], dst_ref=dst.at[c, here, there],
            send_sem=sent[2], recv_sem=recv,
            device_id=(v, lax.rem(p + step, K)), device_id_type=MESH,
        )

    full = pl.ds(0, cols)

    def up_copy(c, i, here=None, there=full):
        return chain_copy(recv_up, c, leg(i) if here is None else here, there, up_recv.at[c - 2, i], 1)

    def dn_copy(c, i, here=None, there=full):
        return chain_copy(recv_dn, c, leg(i) if here is None else here, there, dn_recv.at[c, i], K - 1)

    def up_last(i):
        return chain_copy(recv_up, 1, cut(i), full, last_recv.at[i], 1)

    def dn_last(i):
        return chain_copy(recv_dn, K - 2, cut(i), full, last_recv.at[i], K - 1)

    def send_early(c, i, here=None):
        @pl.when(first & (c >= 2))
        def _():
            up_copy(c, i, here).start()

        @pl.when(last & (c <= K - 3))
        def _():
            dn_copy(c, i, here).start()

    def opening(here, h):
        c = chunk_at(0)
        there = pl.ds(h * half_cols, half_cols)
        part[c, here, there] = jnp.dot(
            tok[here], w[c, :, there], preferred_element_type=jnp.float32
        ).astype(jnp.bfloat16)

        @pl.when(first)
        def _():
            up_copy(c, 0, here, there).start()

        @pl.when(last)
        def _():
            dn_copy(c, 0, here, there).start()

    opening(pl.ds(0, sub), 0)
    tok_sub(1).wait()
    opening(pl.ds(sub, sub), 0)
    w_half(1).wait()
    opening(pl.ds(0, piece), 1)
    gather_a.begin()
    gather_a.second()

    tok_rest.wait()
    base(chunk_at(0), 1)
    send_early(chunk_at(0), 0, cut(1))

    @pl.loop(2, PIECES)
    def _(i):
        base(chunk_at(0), i)

    send_early(chunk_at(0), 1)

    others = w.at[pl.ds(0, K - 1)]
    pltpu.make_async_copy(others, others, w_sem.at[2]).wait()

    @pl.loop(1, K)
    def _(k):
        c = chunk_at(k)

        @pl.loop(0, PIECES)
        def _(i):
            base(c, i)

            @pl.when(i % 2 == 1)
            def _():
                send_early(c, i // 2)

    own_counts.wait()
    running = jnp.int32(0)
    ends[0] = running
    for j in range(V * var_dev):
        running = running + counts_ref[v, j]
        ends[j + 1] = running

    own_b.wait()
    own_scale.wait()
    for j in range(var_dev):
        turned = jnp.broadcast_to(scale_ref[j : j + 1, :].astype(jnp.float32), (R, R)).T
        for q in range(cols // R):
            at = pl.ds(q * R, R)
            b_all[v, j, :, at] = (b_raw[j, :, at].astype(jnp.float32) * turned).astype(jnp.bfloat16)

    def owner_mask(o, j, i, size, n):
        at = lax.broadcasted_iota(jnp.int32, (size, n), 0) + i * size
        return (at >= ends[o * var_dev + j]) & (at < ends[o * var_dev + j + 1])

    def rank_blocks(lo, hi, clear=False):
        @pl.loop(lo, hi)
        def _(d):
            o = lax.bitwise_xor(v, d)
            both = jnp.concatenate([a_all[o, j] for j in range(var_dev)], axis=1)
            product = jnp.dot(tok[...], both, preferred_element_type=jnp.float32)
            picked = rank[...]
            if clear:
                picked = jnp.where(d == lo, jnp.zeros_like(picked), picked)
            for j in range(var_dev):
                picked = jnp.where(owner_mask(o, j, 0, rows, R), product[:, j * R : (j + 1) * R], picked)
            rank[...] = picked

    def add_up(c, i):
        @pl.when((p > 0) & (p < c))
        def _():
            up_copy(c, i).wait_recv()
            for half_leg in range(2):
                here = cut(2 * i + half_leg)
                part[c, here] = (
                    part[c, here].astype(jnp.float32) + recv_up[c, here].astype(jnp.float32)
                ).astype(jnp.bfloat16)
            up_copy(c, i).start()

    def add_dn(c, i):
        @pl.when((p < K - 1) & (p > c))
        def _():
            dn_copy(c, i).wait_recv()
            for half_leg in range(2):
                here = cut(2 * i + half_leg)
                part[c, here] = (
                    part[c, here].astype(jnp.float32) + recv_dn[c, here].astype(jnp.float32)
                ).astype(jnp.bfloat16)
            dn_copy(c, i).start()

    def near(step, i):
        @pl.when(low_half)
        def _():
            add_up(K - 1 - step, i)

        @pl.when(jnp.logical_not(low_half))
        def _():
            add_dn(step, i)

    def far(step, i):
        @pl.when(low_half)
        def _():
            add_dn(step, i)

        @pl.when(jnp.logical_not(low_half))
        def _():
            add_up(K - 1 - step, i)

    more = K > 3
    near(0, 0)
    gather_a.take(0)
    own_a.wait()
    gather_a.take_core(0)
    rank_blocks(0, 2, clear=True)
    near(0, 1)
    for k in range(1, len(chips) - 1):
        gather_a.take(2 * k - 1)
        gather_a.take(2 * k)
    gather_a.take(2 * len(chips) - 3)
    if len(chips) == 2:
        gather_a.take_core(2)
        gather_a.take_core(4)
        rank_blocks(2, 4)
        far(0, 0)
        rank_blocks(4, 6)
    else:
        far(0, 0)
    if more:
        near(1, 0)
    gather_a.take(2 * len(chips) - 2)
    if len(chips) == 2:
        rank_blocks(6, 7)
        gather_a.take_core(6)
        rank_blocks(7, 8)
    else:
        for d in range(2, V, 2):
            gather_a.take_core(d)
        rank_blocks(2, V)

    def rup_copy(i):
        return pltpu.make_async_remote_copy(
            src_ref=rank_send_up.at[leg(i)], dst_ref=rank_up.at[leg(i)],
            send_sem=sent[3], recv_sem=rup_recv.at[i],
            device_id=(v, lax.rem(p + 1, K)), device_id_type=MESH,
        )

    def rdn_copy(i):
        return pltpu.make_async_remote_copy(
            src_ref=rank_send_dn.at[leg(i)], dst_ref=rank_dn.at[leg(i)],
            send_sem=sent[4], recv_sem=rdn_recv.at[i],
            device_id=(v, lax.rem(p + K - 1, K)), device_id_type=MESH,
        )

    @pl.when(first)
    def _():
        rank_send_up[...] = rank[...].astype(jnp.bfloat16)
        for i in range(2):
            rup_copy(i).start()

    @pl.when(last)
    def _():
        rank_send_dn[...] = rank[...].astype(jnp.bfloat16)
        for i in range(2):
            rdn_copy(i).start()

    @pl.when(first)
    def _():
        for i in range(PIECES):
            up_last(i).start()

    @pl.when(last)
    def _():
        for i in range(PIECES):
            dn_last(i).start()

    gather_b.begin()
    gather_b.second()
    far(0, 1)

    def rank_up_step(i):
        @pl.when(p > 0)
        def _():
            rup_copy(i).wait_recv()

            @pl.when(p < K - 1)
            def _():
                rank_send_up[leg(i)] = (
                    rank[leg(i)] + rank_up[leg(i)].astype(jnp.float32)
                ).astype(jnp.bfloat16)
                rup_copy(i).start()

    def rank_dn_step(i):
        @pl.when(p < K - 1)
        def _():
            rdn_copy(i).wait_recv()

            @pl.when(p > 0)
            def _():
                rank_send_dn[leg(i)] = (
                    rank[leg(i)] + rank_dn[leg(i)].astype(jnp.float32)
                ).astype(jnp.bfloat16)
                rdn_copy(i).start()

    def rank_turn(turn):
        @pl.loop(0, 2)
        def _(i):
            @pl.when(low_half if turn == 0 else jnp.logical_not(low_half))
            def _():
                rank_up_step(i)

            @pl.when(jnp.logical_not(low_half) if turn == 0 else low_half)
            def _():
                rank_dn_step(i)

    rank_turn(0)
    gather_b.take(0)
    rank_turn(1)
    if more:
        near(1, 1)
        far(1, 0)
        far(1, 1)
    for step in range(2, K - 2):
        for i in range(2):
            near(step, i)
            far(step, i)
    for k in range(1, len(chips)):
        gather_b.take(k)
    gather_b.take_cores()

    @pl.loop(0, PIECES)
    def _(i):
        @pl.when(p > 0)
        def _():
            rank[cut(i)] += rank_up[cut(i)].astype(jnp.float32)

        @pl.when(p < K - 1)
        def _():
            rank[cut(i)] += rank_dn[cut(i)].astype(jnp.float32)

        low = rank[cut(i)].astype(jnp.bfloat16)
        zero = jnp.zeros_like(low)
        wide = jnp.concatenate(
            [
                jnp.where(owner_mask(o, j, i, piece, R), low, zero)
                for o in range(V)
                for j in range(var_dev)
            ],
            axis=1,
        )
        delta = jnp.dot(
            wide, b_all[...].reshape(V * var_dev * R, cols), preferred_element_type=jnp.float32
        ).astype(jnp.bfloat16)
        total[cut(i)] = delta.astype(jnp.float32) + part[p, cut(i)].astype(jnp.float32)

    def more_up(here):
        total[here] += recv_up[p, here].astype(jnp.float32)

    def more_dn(here):
        total[here] += recv_dn[p, here].astype(jnp.float32)

    @pl.loop(0, PIECES)
    def _(i):
        @pl.when(low_half & (p < K - 1))
        def _():
            @pl.when(i % 2 == 0)
            def _():
                dn_copy(p, i // 2).wait_recv()

            more_dn(cut(i))

        @pl.when(jnp.logical_not(low_half) & (p > 0))
        def _():
            @pl.when(i % 2 == 0)
            def _():
                up_copy(p, i // 2).wait_recv()

            more_up(cut(i))

    gather_a.wait_sent()
    gather_b.wait_sent()

    def wait_sent(src, dst, sem):
        pltpu.make_async_remote_copy(
            src_ref=src, dst_ref=dst, send_sem=sem, recv_sem=last_recv.at[0],
            device_id=(lax.bitwise_xor(v, 1), p), device_id_type=MESH,
        ).wait_send()

    @pl.when(p < K - 1)
    def _():
        wait_sent(rank_send_up, rank_up, sent[3])

    @pl.when(p > 0)
    def _():
        wait_sent(rank_send_dn, rank_dn, sent[4])

    @pl.loop(0, PIECES)
    def _(i):
        @pl.when(low_half & (p > 0))
        def _():
            @pl.when(p == 1)
            def _():
                up_last(i).wait_recv()

            @pl.when((p > 1) & (i % 2 == 0))
            def _():
                up_copy(p, i // 2).wait_recv()

            out[cut(i)] = (total[cut(i)] + recv_up[p, cut(i)].astype(jnp.float32)).astype(jnp.bfloat16)

        @pl.when(jnp.logical_not(low_half) & (p < K - 1))
        def _():
            @pl.when(p == K - 2)
            def _():
                dn_last(i).wait_recv()

            @pl.when((p < K - 2) & (i % 2 == 0))
            def _():
                dn_copy(p, i // 2).wait_recv()

            out[cut(i)] = (total[cut(i)] + recv_dn[p, cut(i)].astype(jnp.float32)).astype(jnp.bfloat16)

        @pl.when(edge)
        def _():
            out[cut(i)] = total[cut(i)].astype(jnp.bfloat16)

    each = pl.ds(0, K - 1)
    wait_sent(part.at[each], recv_up.at[each], sent[2])


def body(V, K, tokens, kv_weight, factor_a, factor_scale, factor_b, counts):
    rows, feats = tokens.shape
    wide = kv_weight.shape[1]
    cols = wide // K
    var_dev, _, R = factor_a.shape
    DMA = pltpu.SemaphoreType.DMA
    bf16, f32 = jnp.bfloat16, jnp.float32
    anywhere = pl.BlockSpec(memory_space=pl.ANY)
    steps = (V // 2).bit_length() - 1
    return pl.pallas_call(
        functools.partial(kernel, V, K),
        out_shape=pltpu.VMEM((rows, cols), bf16),
        in_specs=[
            anywhere, anywhere, anywhere, anywhere, anywhere, anywhere,
        ],
        out_specs=pl.BlockSpec(memory_space=pltpu.VMEM),
        scratch_shapes=[
            pltpu.VMEM((rows, feats), bf16),
            pltpu.VMEM((K, feats, cols), bf16),
            pltpu.VMEM((V, var_dev, feats, R), bf16),
            pltpu.VMEM((var_dev, R, cols), bf16),
            pltpu.VMEM((V, var_dev, R, cols), bf16),
            pltpu.VMEM((K, rows, cols), bf16),
            pltpu.VMEM((K, rows, cols), bf16),
            pltpu.VMEM((K, rows, cols), bf16),
            pltpu.VMEM((rows, R), f32),
            pltpu.VMEM((rows, R), bf16),
            pltpu.VMEM((rows, R), bf16),
            pltpu.VMEM((rows, R), bf16),
            pltpu.VMEM((rows, R), bf16),
            pltpu.VMEM((rows, cols), f32),
            pltpu.VMEM(factor_scale.shape, bf16),
            pltpu.SMEM(counts.shape, jnp.int32),
            pltpu.SMEM((V * var_dev + 1,), jnp.int32),
            DMA((3,)), DMA((3,)), DMA((4,)),
            DMA((2 * steps - 1,)), DMA((V // 2,)), DMA((steps,)), DMA((1,)),
            DMA((K - 2, 2)), DMA((K - 2, 2)), DMA((PIECES,)), DMA((2,)), DMA((2,)),
        ],
        compiler_params=pltpu.CompilerParams(
            collective_id=0, has_side_effects=True, vmem_limit_bytes=60 << 20
        ),
    )(tokens, kv_weight, factor_a, factor_scale, factor_b, counts)


def solution(mesh):
    return jax.shard_map(
        functools.partial(body, mesh.shape["var"], mesh.shape["tp"]),
        mesh=mesh,
        in_specs=(
            P("var", "tp"),
            P("tp", None),
            P("var", "tp", None),
            P("var", None),
            P("var", None, "tp"),
            P(),
        ),
        out_specs=P("var", "tp"),
        check_vma=False,
    )
```
